256 devices in a mesh: gx: 8 (over x, y_hi), gy: 4 (over y_lo, core), gz: 8 (over z).
Axes of the slice: x: 4, y: 4 (y_hi: 2, y_lo: 2; y = y_hi * 2 + y_lo), z: 8, core: 2. Of those that a mesh axis runs over, the one named last changes fastest.
Arguments:
- local_pos: float32 [16, 8, 8, 3, 64], P('gx', 'gy', 'gz'), as said below
- counts: int32 [16, 8, 8], P('gx', 'gy', 'gz'), may hold values from 8 to 64, as said below
- species: int32 [16, 8, 8, 64], P('gx', 'gy', 'gz'), may hold values from 0 to 9
- features: bfloat16 [16, 8, 8, 64, 128], P('gx', 'gy', 'gz'), may hold values from -6 to 6
- radial_weights: float32 [2, 8, 128], replicated, may hold values from -2 to 2
- coupling: float32 [3, 10, 128], replicated, may hold values from -3 to 3
- mixing: float32 [128, 128], replicated, may hold values from -0.5 to 0.5
- hidden_weights: float32 [128, 16], replicated, may hold values from -0.5 to 0.5
- output_weights: float32 [16], replicated, may hold values from -1.5 to 1.5
Outputs:
- atom_energy: float32 [16, 8, 8, 64], P('gx', 'gy', 'gz')
- forces: float32 [16, 8, 8, 3, 64], P('gx', 'gy', 'gz')
- feature_grad: float32 [16, 8, 8, 64, 128], P('gx', 'gy', 'gz')
The draws below stay inside these ranges and needn't reach their ends.
Inputs may be any that keep to these rules, and one draw needn't show every extreme that they name: `counts`: every cell holds between 8 and 64 atoms, and at least one cell is full. `local_pos`: the slots of a cell sit on distinct sites of a 4 x 4 x 4 lattice of spacing 7 / 4, each moved by at most 0.3 spacings along each coordinate, so any two slots are 0.4 spacings apart or more.
All inputs are finite; a program needn't handle non-finite values.
Results may differ from the reference program's by a relative error of at most 0.0048.
Values may be sent and summed in bfloat16 or wider, within the bound.
No kernel may reach another device: no remote copies, remote signals or barrier semaphores. Data moves between devices by JAX's collectives and lax.ppermute only.
A program may use at most 64 MiB of HBM per device.

```python
import jax
import jax.numpy as jnp
import numpy as np
from jax import lax

CHAN = 128
NB = 8
HID = 16
NSPEC = 10
LAT = 4
SLOTS = 64
NCX = 16
NCY = 8
NCZ = 8


def draw_local_pos(key, part):
    total_cells = NCX * NCY * NCZ
    order_key, jitter_key = jax.random.split(key)
    orders = jax.vmap(lambda subkey: jax.random.permutation(subkey, SLOTS))(jax.random.split(order_key, total_cells))
    coord_x = orders // (LAT * LAT)
    coord_y = orders // LAT % LAT
    coord_z = orders % LAT
    lattice = jnp.stack([coord_x, coord_y, coord_z], axis=1).astype(jnp.float32)
    jitter = jax.random.uniform(jitter_key, (total_cells, 3, SLOTS), jnp.float32, -0.3, 0.3)
    spacing = 7.0 / LAT
    return ((lattice + 0.5 + jitter) * spacing).reshape(NCX, NCY, NCZ, 3, SLOTS)


def draw_counts(key, part):
    drawn = jax.random.randint(key, (NCX, NCY, NCZ), SLOTS // 8, SLOTS + 1, jnp.int32)
    return drawn.at[0, 0, 0].set(SLOTS)


def touch_ends(result, stream_key, low, high):
    place = [jax.random.randint(jax.random.fold_in(stream_key, axis), (), 0, length) for axis, length in enumerate(result.shape)]
    main_axis = result.shape.index(max(result.shape))
    neighbour = place[:main_axis] + [(place[main_axis] + 1) % result.shape[main_axis]] + place[main_axis + 1:]
    return result.at[tuple(place)].set(low).at[tuple(neighbour)].set(high)


def levels(key, extent, cuts, low, top_value):
    level, own = 1.0, jax.random.fold_in(key, 6)
    for dim, shards_of in cuts:
        draws = jnp.exp(jax.random.uniform(jax.random.fold_in(own, dim), (shards_of,), jnp.float32, low / len(cuts), top_value / len(cuts)))
        level = level * jnp.repeat(draws, extent[dim] // shards_of).reshape([-1 if axis == dim else 1 for axis in range(len(extent))])
    return level


def scatter_about(rng, dims, spread, limit, pieces=(), kind=jnp.bfloat16):
    loudness = levels(rng, dims, pieces, -0.22, 0.18) if pieces else 1.0
    values = jax.random.normal(rng, dims, jnp.float32) * spread * loudness
    return jnp.minimum(jnp.maximum(values, -limit), limit).astype(kind)


def setup_inputs(seed: int = 0) -> dict:
    seeds = jax.random.split(jax.random.key(seed), 10)
    return {
        "local_pos": draw_local_pos(jax.random.fold_in(seeds[9], 71), 0),
        "counts": draw_counts(jax.random.fold_in(seeds[9], 71), 0),
        "species": touch_ends(jax.random.randint(seeds[2], (NCX, NCY, NCZ, SLOTS), 0, NSPEC), jax.random.fold_in(seeds[2], 1), 0, NSPEC - 1).astype(jnp.int32),
        "features": scatter_about(seeds[3], (NCX, NCY, NCZ, SLOTS, CHAN), 1.0, 6.0, ((0, 8), (1, 4), (2, 8))),
        "radial_weights": scatter_about(seeds[4], (2, NB, CHAN), NB ** -0.5, 2.0, (), jnp.float32),
        "coupling": scatter_about(seeds[5], (3, NSPEC, CHAN), 0.5, 3.0, (), jnp.float32),
        "mixing": scatter_about(seeds[6], (CHAN, CHAN), CHAN ** -0.5, 0.5, (), jnp.float32),
        "hidden_weights": scatter_about(seeds[7], (CHAN, HID), CHAN ** -0.5, 0.5, (), jnp.float32),
        "output_weights": scatter_about(seeds[8], (HID,), HID ** -0.5, 1.5, (), jnp.float32),
    }


SIDE = 7.0
CUTOFF = 5.0
OFFSETS = np.array([[step_a, step_b, step_c] for step_a in (-1, 0, 1) for step_b in (-1, 0, 1) for step_c in (-1, 0, 1)], dtype=np.float32) * SIDE
middle_cell = 13

def edge_terms(own_xyz, far_xyz, pair_weight, self_mask, basis_count):
    displace = far_xyz[:, None, :] - own_xyz[:, :, None]
    radius = jnp.sqrt(lax.optimization_barrier(jnp.sum(displace * displace, axis=0)) + self_mask)
    scaled = radius / CUTOFF
    envelope = 1.0 - 28.0 * scaled ** 6 + 48.0 * scaled ** 7 - 21.0 * scaled ** 8
    envelope = jnp.where(radius < CUTOFF, envelope, 0.0) * pair_weight
    orders = jnp.arange(1, basis_count + 1, dtype=jnp.float32)
    bessel = jnp.sqrt(2.0 / CUTOFF) * jnp.sin(orders[:, None, None] * jnp.pi * radius[None] / CUTOFF) / radius[None]
    radial_part = bessel * envelope[None]
    harmonics = jnp.concatenate([jnp.ones_like(radius)[None], jnp.sqrt(3.0) * displace / radius[None]], axis=0)
    edge_values = radial_part[:, None] * harmonics[None]
    return edge_values.reshape(basis_count * 4, radius.shape[0], radius.shape[1])

def cell_terms(own_pos, own_kind, near_pos, near_feat, radial_weights, coupling, mixing, hidden_weights, output_weights):
    capacity = own_pos.shape[1]
    near_count = near_pos.shape[0] * capacity
    basis_count = radial_weights.shape[1]
    channels = near_feat.shape[1]
    far_xyz = (near_pos[:, :3, :] + OFFSETS[:, :, None]).transpose(1, 0, 2).reshape(3, near_count)
    far_occ = near_pos[:, 3, :].reshape(near_count)
    own_xyz = own_pos[:3]
    own_occ = own_pos[3]
    column = jnp.arange(near_count, dtype=jnp.int32)
    own_index = jnp.arange(capacity, dtype=jnp.int32)
    self_mask = (column[None, :] == own_index[:, None] + middle_cell * capacity).astype(jnp.float32)
    pair_weight = own_occ[:, None] * far_occ[None, :] * (1.0 - self_mask)

    def edges(xyz_own, xyz_far):
        return edge_terms(xyz_own, xyz_far, pair_weight, self_mask, basis_count)
    edge_values, pullback = jax.vjp(edges, own_xyz, far_xyz)
    edge_half = edge_values.astype(jnp.bfloat16).reshape(basis_count * 4 * capacity, near_count)
    summed = jnp.dot(edge_half, near_feat, preferred_element_type=jnp.float32)
    summed = summed.reshape(basis_count, 4, capacity, channels)
    scalar = lax.optimization_barrier(jnp.sum(summed[:, 0] * radial_weights[0][:, None, :], axis=0))
    vector = lax.optimization_barrier(jnp.sum(summed[:, 1:] * radial_weights[1][:, None, None, :], axis=0))
    kind_onehot = (own_kind[:, None] == jnp.arange(coupling.shape[1], dtype=jnp.int32)[None, :]).astype(jnp.float32)
    weights = jnp.einsum('sk,qkc->qsc', kind_onehot, coupling, precision=lax.Precision.HIGHEST)
    length_sq = lax.optimization_barrier(jnp.sum(vector * vector, axis=0))
    product = weights[0] * scalar + weights[1] * scalar * scalar + weights[2] * length_sq
    mixed_out = jnp.dot(product, mixing, precision=lax.Precision.HIGHEST)
    hidden = jnp.dot(mixed_out, hidden_weights, precision=lax.Precision.HIGHEST)
    logistic = jax.nn.sigmoid(hidden)
    energy = own_occ * lax.optimization_barrier(jnp.sum(output_weights[None, :] * hidden * logistic, axis=1))
    d_hidden = own_occ[:, None] * output_weights[None, :] * logistic * (1.0 + hidden * (1.0 - logistic))
    d_mixed = jnp.dot(d_hidden, hidden_weights.T, precision=lax.Precision.HIGHEST)
    d_product = jnp.dot(d_mixed, mixing.T, precision=lax.Precision.HIGHEST)
    d_scalar = d_product * (weights[0] + 2.0 * weights[1] * scalar)
    d_vector = 2.0 * weights[2][None] * vector * d_product[None]
    d_first = radial_weights[0][:, None, :] * d_scalar[None]
    d_rest = radial_weights[1][:, None, None, :] * d_vector[None]
    d_summed = jnp.concatenate([d_first[:, None], d_rest], axis=1)
    d_half = d_summed.astype(jnp.bfloat16).reshape(basis_count * 4 * capacity, channels)
    d_edge = lax.dot_general(d_half, near_feat, (((1,), (1,)), ((), ())), preferred_element_type=jnp.float32)
    d_edge = d_edge.reshape(basis_count * 4, capacity, near_count)
    d_feat = lax.dot_general(edge_half, d_half, (((0,), (0,)), ((), ())), preferred_element_type=jnp.float32)
    d_own, d_far = pullback(d_edge)
    d_far = d_far.reshape(3, near_pos.shape[0], capacity).transpose(1, 0, 2)
    d_far = d_far.at[middle_cell].add(d_own)
    return (energy, d_far, d_feat.reshape(near_pos.shape[0], capacity, channels))

def reference(local_pos, counts, species, features, radial_weights, coupling, mixing, hidden_weights, output_weights):
    cells_x, cells_y, cells_z = counts.shape
    capacity = features.shape[3]
    channels = features.shape[4]
    total_cells = cells_x * cells_y * cells_z
    occupied = (jnp.arange(capacity, dtype=jnp.int32)[None, None, None, :] < counts[..., None]).astype(jnp.float32)
    with_occ = jnp.concatenate([local_pos, occupied[:, :, :, None, :]], axis=3).reshape(total_cells, 4, capacity)
    feat_flat = features.reshape(total_cells, capacity, channels)
    kind_flat = species.reshape(total_cells, capacity)
    flat_ids = np.arange(total_cells)
    coord_x = flat_ids // (cells_y * cells_z)
    coord_y = flat_ids // cells_z % cells_y
    coord_z = flat_ids % cells_z
    columns = []
    for step_x in range(3):
        for step_y in range(3):
            for step_z in range(3):
                columns.append((coord_x + step_x - 1) % cells_x * cells_y * cells_z + (coord_y + step_y - 1) % cells_y * cells_z + (coord_z + step_z - 1) % cells_z)
    neighbor_table = jnp.asarray(np.stack(columns, axis=1).astype(np.int32))

    def visit_cell(totals, cell_id):
        feat_total, pos_total = totals
        near_index = neighbor_table[cell_id]
        near_pos = with_occ[near_index]
        near_feat = feat_flat[near_index].reshape(27 * capacity, channels)
        energy, d_far, d_feat = cell_terms(with_occ[cell_id], kind_flat[cell_id], near_pos, near_feat, radial_weights, coupling, mixing, hidden_weights, output_weights)
        return ((feat_total.at[near_index].add(d_feat), pos_total.at[near_index].add(d_far)), energy)
    start = (jnp.zeros((total_cells, capacity, channels), jnp.float32), jnp.zeros((total_cells, 3, capacity), jnp.float32))
    (feat_total, pos_total), energies = lax.scan(visit_cell, start, jnp.arange(total_cells, dtype=jnp.int32))
    atom_energy = energies.reshape(cells_x, cells_y, cells_z, capacity)
    forces = (-pos_total).reshape(cells_x, cells_y, cells_z, 3, capacity)
    feature_grad = feat_total.reshape(cells_x, cells_y, cells_z, capacity, channels)
    return (atom_energy, forces, feature_grad)
```

```python
import functools

import jax
import jax.numpy as jnp
import numpy as np
from jax import lax
from jax.experimental import pallas as pl
from jax.experimental.pallas import tpu as pltpu
from jax.sharding import PartitionSpec as P

SIDE = 7.0
CUTOFF = 5.0
LAT = 4
SLOTS = LAT**3
NB = 8
CHAN = 128
EXTRA = 8
ROWS = SLOTS + EXTRA
COLROWS = 16
RUN = 3 * COLROWS
INNER = [(a, b) for a in (-1, 0, 1) for b in (-1, 0, 1)]
OUTER = [(a, b) for a in (-2, 2) for b in (-1, 0, 1)] + [(b, a) for a in (-2, 2) for b in (-1, 0, 1)]
WINDOW = []
_at = 0
for _a, _b in INNER:
    WINDOW.append((_a, _b, 4, 40, _at))
    _at += 40
for _a, _b in OUTER:
    WINDOW.append((_a, _b, 8, 32, _at))
    _at += 32
USED = _at
NJ = 768
TILE = 128
FAR = 1000.0


def offset_table():
    table = np.zeros((4, 8, NJ), np.float32)
    table[:, :3, USED:] = FAR
    for parity in range(4):
        px, py = parity // 2, parity % 2
        for a, b, first, count, at in WINDOW:
            table[parity, 0, at : at + count] = SIDE * ((px + a) // 2)
            table[parity, 1, at : at + count] = SIDE * ((py + b) // 2)
            run = np.arange(first, first + count)
            table[parity, 2, at : at + count] = SIDE * (run // COLROWS - 1)
    return table


def pick_table():
    table = np.zeros((8, CHAN), np.float32)
    for group in range(8):
        for part in range(3):
            for comp in range(3):
                table[comp, 16 * group + 3 * part + comp] = 1.0
    return table


def spread_table():
    table = np.zeros((16, CHAN), np.float32)
    for group in range(8):
        for part in range(2):
            for comp in range(3):
                table[3 * part + comp, 16 * group + comp] = 1.0
    return table


def poly_coeffs():
    v = 0.5 * np.cos(np.pi * (np.arange(400) + 0.5) / 400)
    sines = np.polynomial.polynomial.polyfit(v * v, np.sin(np.pi * v) / v, 5)
    cosines = np.polynomial.polynomial.polyfit(v * v, np.cos(np.pi * v), 6)
    return [float(c) for c in sines], [float(c) for c in cosines]


SIN_C, COS_C = poly_coeffs()


def horner(coeffs, x):
    value = coeffs[-1] * x + coeffs[-2]
    for c in coeffs[-3::-1]:
        value = value * x + c
    return value


def dot(a, b, dims, precision=None):
    return lax.dot_general(a, b, (dims, ((), ())), preferred_element_type=jnp.float32, precision=precision)


NN = ((1,), (0,))
NT = ((1,), (1,))
TN = ((0,), (0,))


def site_onehot(pos, count):
    site = jnp.clip(jnp.floor(pos * (LAT / SIDE)).astype(jnp.int32), 0, LAT - 1)
    sx, sy, sz = site[0:1], site[1:2], site[2:3]
    row = (((sx >> 1) * 2 + (sy >> 1)) * 4 + sz) * 4 + (sx & 1) * 2 + (sy & 1)
    slot = lax.broadcasted_iota(jnp.int32, (1, SLOTS), 1)
    row = jnp.where(slot < count, row, -1)
    return lax.broadcasted_iota(jnp.int32, (SLOTS, SLOTS), 0) == row


def lane_group(rows):
    return lax.broadcasted_iota(jnp.int32, (rows, CHAN), 1) >> 4


def sort_kernel(count_ref, pos_ref, kind_ref, feat_ref, msg_ref, parts_ref):
    group = lane_group(EXTRA)
    parts_ref[...] = jnp.zeros_like(parts_ref)
    for cell in range(pos_ref.shape[0]):
        pos = pos_ref[cell]
        hot = site_onehot(pos, count_ref[cell]).astype(jnp.bfloat16)
        first = pos.astype(jnp.bfloat16).astype(jnp.float32)
        left = pos - first
        second = left.astype(jnp.bfloat16).astype(jnp.float32)
        third = left - second
        kind = kind_ref[cell : cell + 1].astype(jnp.float32)
        for g in range(8):
            parts_ref[cell, 16 * g : 16 * g + 3] = first
            parts_ref[cell, 16 * g + 3 : 16 * g + 6] = second
            parts_ref[cell, 16 * g + 6 : 16 * g + 9] = third
            parts_ref[cell, 16 * g + 9 : 16 * g + 10] = kind
            parts_ref[cell, 16 * g + 10 : 16 * g + 11] = jnp.ones_like(kind)
        msg_ref[cell, :SLOTS] = dot(hot, feat_ref[cell], NN).astype(jnp.bfloat16)
        spread = dot(hot, parts_ref[cell].astype(jnp.bfloat16), NT)
        extra = jnp.zeros((EXTRA, CHAN), jnp.float32)
        for g in range(8):
            extra = extra + jnp.where(group == g, spread[8 * g : 8 * g + 8], 0.0)
        msg_ref[cell, SLOTS:] = extra.astype(jnp.bfloat16)


def column_base(x, y):
    return (x * 8 + y) * RUN


def main_kernel(
    own_ref, xl_ref, xh_ref, yl_ref, yh_ref, zl_ref, zh_ref,
    off_ref, pick_ref, spread_ref, rw_ref, coup_ref, mix_ref, hid_ref, ow_ref,
    mid_ref, zlo_ref, zho_ref, energy_ref,
    feat_ext, pos_ext, feat_win, pos_win, edges, saved, sums, d_sums, d_half, d_far,
):
    group8 = lane_group(8)

    def place(ref, cell, cx, cy, cz):
        for cc in range(4):
            base = column_base(2 * cx + cc // 2, 2 * cy + cc % 2) + cz * COLROWS
            base = base if isinstance(base, int) else pl.multiple_of(base, 16)
            feat_ext[pl.ds(base, COLROWS)] = ref[cell, COLROWS * cc : COLROWS * cc + COLROWS].astype(jnp.float32)
            scalars = ref[cell, SLOTS:].astype(jnp.float32)
            for h in range(2):
                pos_ext[pl.ds(base + 8 * h, 8)] = jnp.where(group8 == 2 * cc + h, scalars, 0.0)

    for cell in range(4):
        place(own_ref, cell, 1 + cell // 2, 1 + cell % 2, 1)
        place(yl_ref, cell, cell, 0, 1)
        place(yh_ref, cell, cell, 3, 1)
    for cell in range(2):
        place(xl_ref, cell, 0, 1 + cell, 1)
        place(xh_ref, cell, 3, 1 + cell, 1)

    def place_z(cell, carry):
        place(zl_ref, cell, cell // 4, cell % 4, 0)
        place(zh_ref, cell, cell // 4, cell % 4, 2)
        return carry

    lax.fori_loop(0, 16, place_z, 0)

    lane = lax.broadcasted_iota(jnp.int32, (COLROWS, CHAN), 1) & 15
    pick = pick_ref[...].astype(jnp.bfloat16)
    amp = float(np.sqrt(2.0 / CUTOFF))
    root3 = float(np.sqrt(3.0))

    def own_scalar(rows, lanes):
        return jnp.sum(jnp.where(lanes, rows, 0.0), axis=1, keepdims=True)

    def forward(g, carry):
        gx, gy = g // 4 + 2, g % 4 + 2
        base = column_base(gx, gy)
        for a, b, first, count, at in WINDOW:
            start = base + (a * 8 + b) * RUN + first
            feat_win[g, at : at + count] = feat_ext[pl.ds(start, count)].astype(jnp.bfloat16)
            pos_win[at : at + count] = pos_ext[pl.ds(start, count)].astype(jnp.bfloat16)
        feat_win[g, USED:] = jnp.zeros((NJ - USED, CHAN), jnp.bfloat16)
        pos_win[USED:] = jnp.zeros((NJ - USED, CHAN), jnp.bfloat16)
        own = pos_ext[pl.ds(pl.multiple_of(base + COLROWS, 16), COLROWS)]
        parity = (gx & 1) * 2 + (gy & 1)
        far = dot(pick, pos_win[...], NT) + off_ref[parity]
        coords = [
            own_scalar(own, (lane == c) | (lane == 3 + c) | (lane == 6 + c)) for c in range(3)
        ]
        for t in range(NJ // TILE):
            at = slice(t * TILE, t * TILE + TILE)
            dx, dy, dz = (far[c : c + 1, at] - coords[c] for c in range(3))
            square = dx * dx + dy * dy + dz * dz
            clear = jnp.maximum(square, 0.25)
            inv = lax.rsqrt(clear)
            u = jnp.minimum(clear * inv * (1.0 / CUTOFF), 1.0)
            inside = (square >= 0.25) & (square < CUTOFF * CUTOFF)
            v = u - 0.5
            v2 = v * v
            sine = horner(COS_C, v2)
            cosine = -(horner(SIN_C, v2) * v)
            u2 = u * u
            u4 = u2 * u2
            u5 = u4 * u
            env = 1.0 + u4 * u2 * (u * (48.0 - 21.0 * u) - 28.0)
            env = jnp.where(inside, env, 0.0)
            slope = (-168.0 / CUTOFF) * u5 * ((1.0 - u) * (1.0 - u))
            slope = jnp.where(inside, slope, 0.0) - env * inv
            ux, uy, uz = dx * inv, dy * inv, dz * inv
            saved[g, 0, :, at] = ux
            saved[g, 1, :, at] = uy
            saved[g, 2, :, at] = uz
            saved[g, 3, :, at] = inv
            saved[g, 4, :, at] = sine
            saved[g, 5, :, at] = cosine
            saved[g, 6, :, at] = env
            saved[g, 7, :, at] = slope
            yx, yy, yz = root3 * ux, root3 * uy, root3 * uz
            twice = 2.0 * cosine
            before = jnp.zeros_like(env)
            radial = amp * sine * inv * env
            for b in range(NB):
                r0 = b * 4 * COLROWS
                edges[g, r0 : r0 + 16, at] = radial.astype(jnp.bfloat16)
                edges[g, r0 + 16 : r0 + 32, at] = (radial * yx).astype(jnp.bfloat16)
                edges[g, r0 + 32 : r0 + 48, at] = (radial * yy).astype(jnp.bfloat16)
                edges[g, r0 + 48 : r0 + 64, at] = (radial * yz).astype(jnp.bfloat16)
                before, radial = radial, twice * radial - before
        summed = dot(edges[g], feat_win[g], NN)
        for m in range(4):
            total = jnp.zeros((COLROWS, CHAN), jnp.float32)
            for b in range(NB):
                r0 = (b * 4 + m) * COLROWS
                total = total + rw_ref[min(m, 1), b : b + 1] * summed[r0 : r0 + 16]
            sums[m, pl.ds(pl.multiple_of(g * COLROWS, 16), COLROWS)] = total
        return carry

    lax.fori_loop(0, 16, forward, 0)

    high = lax.Precision.HIGHEST
    head = dot(mix_ref[...], hid_ref[...], NN, high)
    ow = ow_ref[...]

    def readout(k, carry):
        kinds, occs = [], []
        for s in range(4):
            g = k * 4 + s
            start = column_base(g // 4 + 2, g % 4 + 2) + COLROWS
            own = pos_ext[pl.ds(pl.multiple_of(start, 16), COLROWS)]
            kinds.append(own_scalar(own, lane == 9))
            occs.append(own_scalar(own, lane == 10))
        kind = jnp.concatenate(kinds, axis=0)
        occ = jnp.concatenate(occs, axis=0)
        rows = pl.ds(pl.multiple_of(k * 64, 64), 64)
        scalar = sums[0, rows]
        vectors = [sums[m, rows] for m in (1, 2, 3)]
        weights = []
        for q in range(3):
            w = jnp.zeros((64, CHAN), jnp.float32)
            for s in range(coup_ref.shape[1]):
                w = jnp.where(kind == float(s), coup_ref[q, s : s + 1], w)
            weights.append(w)
        length = vectors[0] * vectors[0] + vectors[1] * vectors[1] + vectors[2] * vectors[2]
        product = weights[0] * scalar + weights[1] * scalar * scalar + weights[2] * length
        hidden = dot(product, head, NN, high)
        logistic = jax.nn.sigmoid(hidden)
        energy = occ * jnp.sum(ow * hidden * logistic, axis=1, keepdims=True)
        energy_ref[rows] = jnp.broadcast_to(energy, (64, CHAN))
        d_hidden = occ * ow * logistic * (1.0 + hidden * (1.0 - logistic))
        d_product = dot(d_hidden, head, NT, high)
        d_sums[0, rows] = d_product * (weights[0] + 2.0 * weights[1] * scalar)
        for m in range(3):
            d_sums[m + 1, rows] = 2.0 * weights[2] * vectors[m] * d_product
        return carry

    lax.fori_loop(0, 4, readout, 0)

    feat_ext[...] = jnp.zeros_like(feat_ext)
    d_pos = pos_ext
    d_pos[...] = jnp.zeros_like(d_pos)
    spread = spread_ref[...].astype(jnp.bfloat16)
    d_far[...] = jnp.zeros_like(d_far)

    def backward(g, carry):
        base = column_base(g // 4 + 2, g % 4 + 2)
        rows = pl.ds(pl.multiple_of(g * COLROWS, 16), COLROWS)
        for m in range(4):
            d_sum = d_sums[m, rows]
            for b in range(NB):
                r0 = (b * 4 + m) * COLROWS
                d_half[r0 : r0 + 16] = (rw_ref[min(m, 1), b : b + 1] * d_sum).astype(jnp.bfloat16)
        totals = [jnp.zeros((COLROWS, TILE), jnp.float32)] * 3
        for t in range(NJ // TILE):
            at = slice(t * TILE, t * TILE + TILE)
            d_edge = dot(d_half[...], feat_win[g, at], NT)
            ux, uy, uz, inv, sine, cosine, env, slope = (saved[g, k, :, at] for k in range(8))
            yx, yy, yz = root3 * ux, root3 * uy, root3 * uz
            twice = 2.0 * cosine
            s_old, s_now = jnp.zeros_like(sine), sine
            c_old, c_now = jnp.ones_like(sine), cosine
            s_sum, c_sum = 0.0, 0.0
            grads = [0.0, 0.0, 0.0]
            for b in range(NB):
                r0 = b * 4 * COLROWS
                e0, e1, e2, e3 = (d_edge[r0 + 16 * m : r0 + 16 * m + 16] for m in range(4))
                w = e0 + yx * e1 + yy * e2 + yz * e3
                s_sum = s_sum + w * s_now
                c_sum = c_sum + w * (c_now * float(b + 1))
                grads = [grads[0] + e1 * s_now, grads[1] + e2 * s_now, grads[2] + e3 * s_now]
                if b + 1 < NB:
                    s_old, s_now = s_now, twice * s_now - s_old
                    c_old, c_now = c_now, twice * c_now - c_old
            scale = amp * inv
            along = scale * (float(np.pi / CUTOFF) * env * c_sum + slope * s_sum)
            across = (root3 * scale) * env * inv
            inner = grads[0] * ux + grads[1] * uy + grads[2] * uz
            along = along - across * inner
            ds = [along * ux + across * grads[0], along * uy + across * grads[1], along * uz + across * grads[2]]
            for c in range(3):
                totals[c] = totals[c] + ds[c]
                column = jnp.sum(ds[c], axis=0, keepdims=True)
                hi = column.astype(jnp.bfloat16)
                d_far[c : c + 1, at] = hi
                d_far[3 + c : 4 + c, at] = (column - hi.astype(jnp.float32)).astype(jnp.bfloat16)
        d_feat = dot(edges[g], d_half[...], TN)
        d_spread = dot(d_far[...], spread, TN)
        for a, b, first, count, at in WINDOW:
            start = pl.ds(base + (a * 8 + b) * RUN + first, count)
            feat_ext[start] = feat_ext[start] + d_feat[at : at + count]
            d_pos[start] = d_pos[start] + d_spread[at : at + count]
        mine = pl.ds(pl.multiple_of(base + COLROWS, 16), COLROWS)
        back = jnp.zeros((COLROWS, CHAN), jnp.float32)
        for c in range(3):
            back = jnp.where(lane == c, jnp.sum(totals[c], axis=1, keepdims=True), back)
        d_pos[mine] = d_pos[mine] - back
        return carry

    lax.fori_loop(0, 16, backward, 0)

    def collect(cell, carry):
        for cz, out in ((0, zlo_ref), (1, mid_ref), (2, zho_ref)):
            scalars = jnp.zeros((EXTRA, CHAN), jnp.float32)
            for cc in range(4):
                base = column_base(2 * (cell // 4) + cc // 2, 2 * (cell % 4) + cc % 2) + cz * COLROWS
                base = pl.multiple_of(base, 16)
                out[cell, COLROWS * cc : COLROWS * cc + COLROWS] = feat_ext[pl.ds(base, COLROWS)].astype(out.dtype)
                for h in range(2):
                    scalars = scalars + jnp.where(group8 == 2 * cc + h, d_pos[pl.ds(base + 8 * h, 8)], 0.0)
            out[cell, SLOTS:] = scalars.astype(out.dtype)
        return carry

    lax.fori_loop(0, 16, collect, 0)


def finish_kernel(count_ref, pos_ref, mid_ref, low_ref, high_ref, energy_ref, e_ref, f_ref, g_ref):
    for cell in range(4):
        hot = site_onehot(pos_ref[cell], count_ref[cell]).astype(jnp.float32)
        arrived = low_ref[cell] if cell < 2 else high_ref[cell - 2]
        total = mid_ref[cell] + arrived.astype(jnp.float32)
        turned = hot.T.astype(jnp.bfloat16)
        rest = total[:SLOTS]
        grad = jnp.zeros((SLOTS, CHAN), jnp.float32)
        for _ in range(3):
            piece = rest.astype(jnp.bfloat16)
            grad = grad + dot(turned, piece, NN)
            rest = rest - piece.astype(jnp.float32)
        g_ref[cell] = grad
        lane = lax.broadcasted_iota(jnp.int32, (EXTRA, CHAN), 1)
        for c in range(3):
            column = jnp.concatenate(
                [
                    jnp.sum(jnp.where(lane == 16 * g + c, total[SLOTS:], 0.0), axis=1, keepdims=True)
                    for g in range(8)
                ],
                axis=0,
            )
            f_ref[cell, c : c + 1] = -jnp.sum(hot * column, axis=0, keepdims=True)
        pieces = []
        for cc in range(4):
            g = (2 * (cell // 2) + cc // 2) * 4 + 2 * (cell % 2) + cc % 2
            pieces.append(energy_ref[g * COLROWS : g * COLROWS + COLROWS, 0:1])
        e_ref[cell : cell + 1] = jnp.sum(hot * jnp.concatenate(pieces, axis=0), axis=0, keepdims=True)


SMEM = pl.BlockSpec(memory_space=pltpu.SMEM)
VMEM = pl.BlockSpec(memory_space=pltpu.VMEM)


def shifted(low_part, high_part, axis):
    count = lax.axis_size(axis)
    up = [(i, (i + 1) % count) for i in range(count)]
    down = [(target, source) for source, target in up]
    from_below = lax.ppermute(high_part, axis, up)
    from_above = lax.ppermute(low_part, axis, down)
    return from_below, from_above


def body(local_pos, counts, species, features, radial_weights, coupling, mixing, hidden_weights, output_weights):
    cells = 4
    pos = local_pos.reshape(cells, 3, SLOTS)
    count = counts.reshape(cells)
    bf16, f32 = jnp.bfloat16, jnp.float32
    own = pl.pallas_call(
        sort_kernel,
        name="sort",
        out_shape=jax.ShapeDtypeStruct((cells, ROWS, CHAN), bf16),
        in_specs=[SMEM, VMEM, VMEM, VMEM],
        out_specs=VMEM,
        scratch_shapes=[pltpu.VMEM((cells, CHAN, SLOTS), f32)],
    )(count, pos, species.reshape(cells, SLOTS), features.reshape(cells, SLOTS, CHAN))
    block = own.reshape(2, 2, ROWS, CHAN)
    xl, xh = shifted(block[:1], block[1:], "gx")
    wide = jnp.concatenate([xl, block, xh], axis=0)
    yl, yh = shifted(wide[:, :1], wide[:, 1:], "gy")
    layer = jnp.concatenate([yl, wide, yh], axis=1)
    zl, zh = shifted(layer, layer, "gz")

    sixteen = jax.ShapeDtypeStruct((16, ROWS, CHAN), bf16)
    mid, z_low, z_high, energy = pl.pallas_call(
        main_kernel,
        name="pairs",
        out_shape=(
            jax.ShapeDtypeStruct((16, ROWS, CHAN), f32),
            sixteen,
            sixteen,
            jax.ShapeDtypeStruct((16 * COLROWS, CHAN), f32),
        ),
        in_specs=[VMEM] * 15,
        out_specs=(VMEM,) * 4,
        scratch_shapes=[
            pltpu.VMEM((64 * RUN, CHAN), f32),
            pltpu.VMEM((64 * RUN, CHAN), f32),
            pltpu.VMEM((16, NJ, CHAN), bf16),
            pltpu.VMEM((NJ, CHAN), bf16),
            pltpu.VMEM((16, 4 * NB * COLROWS, NJ), bf16),
            pltpu.VMEM((16, 8, COLROWS, NJ), f32),
            pltpu.VMEM((4, 16 * COLROWS, CHAN), f32),
            pltpu.VMEM((4, 16 * COLROWS, CHAN), f32),
            pltpu.VMEM((4 * NB * COLROWS, CHAN), bf16),
            pltpu.VMEM((16, NJ), bf16),
        ],
        compiler_params=pltpu.CompilerParams(vmem_limit_bytes=56 << 20),
    )(
        own,
        xl.reshape(2, ROWS, CHAN),
        xh.reshape(2, ROWS, CHAN),
        yl.reshape(4, ROWS, CHAN),
        yh.reshape(4, ROWS, CHAN),
        zl.reshape(16, ROWS, CHAN),
        zh.reshape(16, ROWS, CHAN),
        jnp.asarray(offset_table()),
        jnp.asarray(pick_table()),
        jnp.asarray(spread_table()),
        radial_weights,
        coupling,
        mixing,
        hidden_weights,
        output_weights.reshape(1, -1),
    )
    from_below, from_above = shifted(z_low, z_high, "gz")
    plane = (mid + from_below.astype(f32) + from_above.astype(f32)).reshape(4, 4, ROWS, CHAN)
    from_below, from_above = shifted(plane[:, :1].astype(bf16), plane[:, 3:].astype(bf16), "gy")
    rows = plane[:, 1:3] + jnp.concatenate([from_below, from_above], axis=1).astype(f32)
    from_below, from_above = shifted(rows[:1].astype(bf16), rows[3:].astype(bf16), "gx")
    atom_energy, forces, feature_grad = pl.pallas_call(
        finish_kernel,
        name="finish",
        out_shape=(
            jax.ShapeDtypeStruct((cells, SLOTS), f32),
            jax.ShapeDtypeStruct((cells, 3, SLOTS), f32),
            jax.ShapeDtypeStruct((cells, SLOTS, CHAN), f32),
        ),
        in_specs=[SMEM] + [VMEM] * 5,
        out_specs=(VMEM,) * 3,
    )(
        count,
        pos,
        rows[1:3].reshape(cells, ROWS, CHAN),
        from_below.reshape(2, ROWS, CHAN),
        from_above.reshape(2, ROWS, CHAN),
        energy,
    )
    return (
        atom_energy.reshape(species.shape),
        forces.reshape(local_pos.shape),
        feature_grad.reshape(features.shape),
    )


def solution(mesh):
    placed = (
        P("gx", "gy", "gz", None, None),
        P("gx", "gy", "gz"),
        P("gx", "gy", "gz", None),
        P("gx", "gy", "gz", None, None),
        P(),
        P(),
        P(),
        P(),
        P(),
    )
    return jax.shard_map(
        body,
        mesh=mesh,
        in_specs=placed,
        out_specs=(
            P("gx", "gy", "gz", None),
            P("gx", "gy", "gz", None, None),
            P("gx", "gy", "gz", None, None),
        ),
        check_vma=False,
    )
```

```python
import functools

import jax
import jax.numpy as jnp
import numpy as np
from jax import lax
from jax.experimental import pallas as pl
from jax.experimental.pallas import tpu as pltpu
from jax.sharding import PartitionSpec as P

SIDE = 7.0
CUTOFF = 5.0
LAT = 4
SLOTS = LAT**3
NB = 8
CHAN = 128
EXTRA = 8
ROWS = SLOTS + EXTRA
COLROWS = 16
RUN = 3 * COLROWS
INNER = [(a, b) for a in (-1, 0, 1) for b in (-1, 0, 1)]
OUTER = [(a, b) for a in (-2, 2) for b in (-1, 0, 1)] + [(b, a) for a in (-2, 2) for b in (-1, 0, 1)]
NEAR, REST = [], []
_at = 0
for _a, _b in INNER + OUTER[:7]:
    NEAR.append((_a, _b, COLROWS, COLROWS, _at))
    _at += COLROWS
NJ_NEAR = _at
_at = 0
for _a, _b in OUTER[7:]:
    REST.append((_a, _b, COLROWS, COLROWS, _at))
    _at += COLROWS
for _first, _inner, _count in ((8, False, 8), (32, False, 8), (4, True, 12), (32, True, 12)):
    for _a, _b in INNER if _inner else OUTER:
        REST.append((_a, _b, _first, _count, _at))
        _at += _count
USED = _at
NJ_REST = 512
TILE = 128
FAR = 1000.0
GROUPS = 16
TERMS = 4 * NB * COLROWS


def offset_table(pieces, size):
    table = np.zeros((4, 8, size), np.float32)
    used = sum(piece[3] for piece in pieces)
    table[:, :3, used:] = FAR
    for parity in range(4):
        px, py = parity // 2, parity % 2
        for a, b, first, count, at in pieces:
            table[parity, 0, at : at + count] = SIDE * ((px + a) // 2)
            table[parity, 1, at : at + count] = SIDE * ((py + b) // 2)
            run = np.arange(first, first + count)
            table[parity, 2, at : at + count] = SIDE * (run // COLROWS - 1)
    return table


def pick_table():
    table = np.zeros((8, CHAN), np.float32)
    for group in range(8):
        for part in range(3):
            for comp in range(3):
                table[comp, 16 * group + 3 * part + comp] = 1.0
    return table


def spread_table():
    table = np.zeros((16, CHAN), np.float32)
    for group in range(8):
        for part in range(2):
            for comp in range(3):
                table[3 * part + comp, 16 * group + comp] = 1.0
    return table


def poly_coeffs():
    v = 0.5 * np.cos(np.pi * (np.arange(400) + 0.5) / 400)
    sines = np.polynomial.polynomial.polyfit(v * v, np.sin(np.pi * v) / v, 5)
    cosines = np.polynomial.polynomial.polyfit(v * v, np.cos(np.pi * v), 6)
    return [float(c) for c in sines], [float(c) for c in cosines]


SIN_C, COS_C = poly_coeffs()


def horner(coeffs, x):
    value = coeffs[-1] * x + coeffs[-2]
    for c in coeffs[-3::-1]:
        value = value * x + c
    return value


def dot(a, b, dims, precision=None):
    return lax.dot_general(a, b, (dims, ((), ())), preferred_element_type=jnp.float32, precision=precision)


NN = ((1,), (0,))
NT = ((1,), (1,))
TN = ((0,), (0,))


def site_onehot(pos, count):
    sx, sy, sz = (jnp.clip(jnp.floor(p * (LAT / SIDE)).astype(jnp.int32), 0, LAT - 1) for p in pos)
    row = (((sx >> 1) * 2 + (sy >> 1)) * 4 + sz) * 4 + (sx & 1) * 2 + (sy & 1)
    slot = lax.broadcasted_iota(jnp.int32, (1, SLOTS), 1)
    row = jnp.where(slot < count, row, -1)
    return lax.broadcasted_iota(jnp.int32, (SLOTS, SLOTS), 0) == row


def lane_group(rows):
    return lax.broadcasted_iota(jnp.int32, (rows, CHAN), 1) >> 4


def sort_kernel(count_hbm, pos_hbm, kind_hbm, feat_hbm, low_ref, high_ref, parts_ref, count_ref, pos_ref, kind_ref, feat_ref, sem):
    copies = [
        pltpu.make_async_copy(source, target, sem.at[k])
        for k, (source, target) in enumerate(
            ((count_hbm, count_ref), (pos_hbm, pos_ref), (kind_hbm, kind_ref), (feat_hbm, feat_ref))
        )
    ]
    for copy in copies:
        copy.start()
    group = lane_group(EXTRA)
    parts_ref[...] = jnp.zeros_like(parts_ref)
    for copy in copies:
        copy.wait()
    for cell in range(4):
        x, y = cell // 2, cell % 2
        pos = [pos_ref[3 * cell + c] for c in range(3)]
        hot = site_onehot(pos, count_ref[x, 0, y]).astype(jnp.bfloat16)
        lines = []
        for left in pos:
            first = left.astype(jnp.bfloat16).astype(jnp.float32)
            left = left - first
            second = left.astype(jnp.bfloat16).astype(jnp.float32)
            lines.append((first, second, left - second))
        kind = kind_ref[cell].astype(jnp.float32)
        for g in range(8):
            for part in range(3):
                for c in range(3):
                    at = 16 * g + 3 * part + c
                    parts_ref[cell, at : at + 1] = lines[c][part]
            parts_ref[cell, 16 * g + 9 : 16 * g + 10] = kind
            parts_ref[cell, 16 * g + 10 : 16 * g + 11] = jnp.ones_like(kind)
        out = high_ref if x else low_ref
        out[y, :SLOTS] = dot(hot, feat_ref[cell], NN).astype(jnp.bfloat16)
        spread = dot(hot, parts_ref[cell].astype(jnp.bfloat16), NT)
        extra = jnp.zeros((EXTRA, CHAN), jnp.float32)
        for g in range(8):
            extra = extra + jnp.where(group == g, spread[8 * g : 8 * g + 8], 0.0)
        out[y, SLOTS:] = extra.astype(jnp.bfloat16)


def place(msg, cell, feat_ext, pos_ext, run, shift):
    group = lane_group(8)
    scalars = msg[cell, SLOTS:].astype(jnp.float32)
    for cc in range(4):
        x, y = 2 * (cell % 4) + cc // 2, 2 * (cell // 4) + cc % 2
        base = pl.multiple_of((x * 8 + y) * run + shift, COLROWS)
        feat_ext[pl.ds(base, COLROWS)] = msg[cell, COLROWS * cc : COLROWS * cc + COLROWS].astype(jnp.float32)
        for h in range(2):
            pos_ext[pl.ds(base + 8 * h, 8)] = jnp.where(group == 2 * cc + h, scalars, 0.0)


def column(g, run):
    return ((g // 4 + 2) * 8 + g % 4 + 2) * run


def own_scalar(rows, lanes):
    return jnp.sum(jnp.where(lanes, rows, 0.0), axis=1, keepdims=True)


def lane_kind():
    return lax.broadcasted_iota(jnp.int32, (COLROWS, CHAN), 1) & 15


AMP = float(np.sqrt(2.0 / CUTOFF))
ROOT3 = float(np.sqrt(3.0))


def take_window(g, pieces, run, skip, feat_ext, pos_ext, feat_win, pos_win):
    base = column(g, run)
    for a, b, first, count, at in pieces:
        start = base + (a * 8 + b) * run + first - skip
        feat_win[g, at : at + count] = feat_ext[pl.ds(start, count)].astype(jnp.bfloat16)
        pos_win[at : at + count] = pos_ext[pl.ds(start, count)].astype(jnp.bfloat16)
    own = pos_ext[pl.ds(pl.multiple_of(base + COLROWS - skip, COLROWS), COLROWS)]
    return own


def edge_columns(g, own, far, edges, saved, size):
    lane = lane_kind()
    coords = [own_scalar(own, (lane == c) | (lane == 3 + c) | (lane == 6 + c)) for c in range(3)]
    for t in range(size // TILE):
        at = slice(t * TILE, t * TILE + TILE)
        dx, dy, dz = (far[c : c + 1, at] - coords[c] for c in range(3))
        square = dx * dx + dy * dy + dz * dz
        clear = jnp.maximum(square, 0.25)
        inv = lax.rsqrt(clear)
        u = jnp.minimum(clear * inv * (1.0 / CUTOFF), 1.0)
        inside = (square >= 0.25) & (square < CUTOFF * CUTOFF)
        v = u - 0.5
        v2 = v * v
        sine = horner(COS_C, v2)
        cosine = -(horner(SIN_C, v2) * v)
        u2 = u * u
        u4 = u2 * u2
        u5 = u4 * u
        env = 1.0 + u4 * u2 * (u * (48.0 - 21.0 * u) - 28.0)
        env = jnp.where(inside, env, 0.0)
        slope = (-168.0 / CUTOFF) * u5 * ((1.0 - u) * (1.0 - u))
        slope = jnp.where(inside, slope, 0.0) - env * inv
        ux, uy, uz = dx * inv, dy * inv, dz * inv
        for k, value in enumerate((ux, uy, uz, inv, sine, cosine, env, slope)):
            saved[g, k, :, at] = value
        yx, yy, yz = ROOT3 * ux, ROOT3 * uy, ROOT3 * uz
        twice = 2.0 * cosine
        before = jnp.zeros_like(env)
        radial = AMP * sine * inv * env
        for b in range(NB):
            r0 = b * 4 * COLROWS
            edges[g, r0 : r0 + 16, at] = radial.astype(jnp.bfloat16)
            edges[g, r0 + 16 : r0 + 32, at] = (radial * yx).astype(jnp.bfloat16)
            edges[g, r0 + 32 : r0 + 48, at] = (radial * yy).astype(jnp.bfloat16)
            edges[g, r0 + 48 : r0 + 64, at] = (radial * yz).astype(jnp.bfloat16)
            before, radial = radial, twice * radial - before


def group_rows(g):
    return pl.ds(pl.multiple_of(g * COLROWS, COLROWS), COLROWS)


def contract(g, edges, feat_win, rw_ref, sums, start_ref=None):
    summed = dot(edges[g], feat_win[g], NN)
    rows = group_rows(g)
    for m in range(4):
        total = jnp.zeros((COLROWS, CHAN), jnp.float32) if start_ref is None else start_ref[m, rows]
        for b in range(NB):
            r0 = (b * 4 + m) * COLROWS
            total = total + rw_ref[min(m, 1), b : b + 1] * summed[r0 : r0 + 16]
        sums[m, rows] = total


def back_group(g, size, pieces, run, skip, edges, feat_win, saved, d_sums, rw_ref, spread, d_half, d_far, d_feat_ext, d_pos_ext):
    lane = lane_kind()
    base = column(g, run)
    rows = group_rows(g)
    for m in range(4):
        d_sum = d_sums[m, rows]
        for b in range(NB):
            r0 = (b * 4 + m) * COLROWS
            d_half[r0 : r0 + 16] = (rw_ref[min(m, 1), b : b + 1] * d_sum).astype(jnp.bfloat16)
    totals = [jnp.zeros((COLROWS, TILE), jnp.float32)] * 3
    for t in range(size // TILE):
        at = slice(t * TILE, t * TILE + TILE)
        d_edge = dot(d_half[...], feat_win[g, at], NT)
        ux, uy, uz, inv, sine, cosine, env, slope = (saved[g, k, :, at] for k in range(8))
        yx, yy, yz = ROOT3 * ux, ROOT3 * uy, ROOT3 * uz
        twice = 2.0 * cosine
        s_old, s_now = jnp.zeros_like(sine), sine
        c_old, c_now = jnp.ones_like(sine), cosine
        s_sum, c_sum = 0.0, 0.0
        grads = [0.0, 0.0, 0.0]
        for b in range(NB):
            r0 = b * 4 * COLROWS
            e0, e1, e2, e3 = (d_edge[r0 + 16 * m : r0 + 16 * m + 16] for m in range(4))
            w = e0 + yx * e1 + yy * e2 + yz * e3
            s_sum = s_sum + w * s_now
            c_sum = c_sum + w * (c_now * float(b + 1))
            grads = [grads[0] + e1 * s_now, grads[1] + e2 * s_now, grads[2] + e3 * s_now]
            if b + 1 < NB:
                s_old, s_now = s_now, twice * s_now - s_old
                c_old, c_now = c_now, twice * c_now - c_old
        scale = AMP * inv
        along = scale * (float(np.pi / CUTOFF) * env * c_sum + slope * s_sum)
        across = (ROOT3 * scale) * env * inv
        inner = grads[0] * ux + grads[1] * uy + grads[2] * uz
        along = along - across * inner
        ds = [along * ux + across * grads[0], along * uy + across * grads[1], along * uz + across * grads[2]]
        for c in range(3):
            totals[c] = totals[c] + ds[c]
            far_sum = jnp.sum(ds[c], axis=0, keepdims=True)
            hi = far_sum.astype(jnp.bfloat16)
            d_far[c : c + 1, at] = hi
            d_far[3 + c : 4 + c, at] = (far_sum - hi.astype(jnp.float32)).astype(jnp.bfloat16)
    d_feat = dot(edges[g], d_half[...], TN)
    d_spread = dot(d_far[...], spread, TN)
    for a, b, first, count, at in pieces:
        start = pl.ds(base + (a * 8 + b) * run + first - skip, count)
        d_feat_ext[start] = d_feat_ext[start] + d_feat[at : at + count]
        d_pos_ext[start] = d_pos_ext[start] + d_spread[at : at + count]
    mine = pl.ds(pl.multiple_of(base + COLROWS - skip, COLROWS), COLROWS)
    back = jnp.zeros((COLROWS, CHAN), jnp.float32)
    for c in range(3):
        back = jnp.where(lane == c, jnp.sum(totals[c], axis=1, keepdims=True), back)
    d_pos_ext[mine] = d_pos_ext[mine] - back


def collect(cell, outs, d_feat_ext, d_pos_ext, run):
    group = lane_group(8)
    for shift, out, more in outs:
        scalars = jnp.zeros((EXTRA, CHAN), jnp.float32)
        for cc in range(4):
            x, y = 2 * (cell % 4) + cc // 2, 2 * (cell // 4) + cc % 2
            base = pl.multiple_of((x * 8 + y) * run + shift, COLROWS)
            rows = d_feat_ext[pl.ds(base, COLROWS)]
            if more is not None:
                rows = rows + more[cell, COLROWS * cc : COLROWS * cc + COLROWS]
            out[cell, COLROWS * cc : COLROWS * cc + COLROWS] = rows.astype(out.dtype)
            for h in range(2):
                scalars = scalars + jnp.where(group == 2 * cc + h, d_pos_ext[pl.ds(base + 8 * h, 8)], 0.0)
        if more is not None:
            scalars = scalars + more[cell, SLOTS:]
        out[cell, SLOTS:] = scalars.astype(out.dtype)


def near_kernel(layer_ref, off_ref, pick_ref, rw_ref, sums, feat_win, edges, saved, feat_ext, pos_ext, pos_win):
    def spread_cell(cell, carry):
        place(layer_ref, cell, feat_ext, pos_ext, COLROWS, 0)
        return carry

    lax.fori_loop(0, 16, spread_cell, 0)
    pick = pick_ref[...].astype(jnp.bfloat16)

    def forward(k, carry):
        for g in (4 * k, 4 * k + 1, 4 * k + 2, 4 * k + 3):
            own = take_window(g, NEAR, COLROWS, COLROWS, feat_ext, pos_ext, feat_win, pos_win)
            parity = ((g // 4) & 1) * 2 + (g & 1)
            far = dot(pick, pos_win[...], NT) + off_ref[parity]
            edge_columns(g, own, far, edges, saved, NJ_NEAR)
        for g in (4 * k, 4 * k + 1, 4 * k + 2, 4 * k + 3):
            contract(g, edges, feat_win, rw_ref, sums)
        return carry

    lax.fori_loop(0, GROUPS // 4, forward, 0)


def rest_kernel(
    layer_ref, zl_ref, zh_ref, near_sums, off_ref, pick_ref, spread_ref, rw_ref, coup_ref, mix_ref, hid_ref, ow_ref,
    zlo_ref, zho_ref, mid_ref, energy_ref, d_sums,
    feat_ext, pos_ext, feat_win, pos_win, edges, saved, sums, d_half, d_far,
):
    def spread_cell(cell, carry):
        place(layer_ref, cell, feat_ext, pos_ext, RUN, COLROWS)
        place(zl_ref, cell, feat_ext, pos_ext, RUN, 0)
        place(zh_ref, cell, feat_ext, pos_ext, RUN, 2 * COLROWS)
        return carry

    lax.fori_loop(0, 16, spread_cell, 0)
    pick = pick_ref[...].astype(jnp.bfloat16)
    lane = lane_kind()
    pos_win[USED:] = jnp.zeros((NJ_REST - USED, CHAN), jnp.bfloat16)

    def forward(k, carry):
        for g in (4 * k, 4 * k + 1, 4 * k + 2, 4 * k + 3):
            own = take_window(g, REST, RUN, 0, feat_ext, pos_ext, feat_win, pos_win)
            feat_win[g, USED:] = jnp.zeros((NJ_REST - USED, CHAN), jnp.bfloat16)
            parity = ((g // 4) & 1) * 2 + (g & 1)
            far = dot(pick, pos_win[...], NT) + off_ref[parity]
            edge_columns(g, own, far, edges, saved, NJ_REST)
        for g in (4 * k, 4 * k + 1, 4 * k + 2, 4 * k + 3):
            contract(g, edges, feat_win, rw_ref, sums, near_sums)
        return carry

    lax.fori_loop(0, GROUPS // 4, forward, 0)

    high = lax.Precision.HIGHEST
    head = dot(mix_ref[...], hid_ref[...], NT, high)
    ow = ow_ref[...]

    def readout(k, carry):
        kinds, occs = [], []
        for s in range(4):
            start = column(k * 4 + s, RUN) + COLROWS
            own = pos_ext[pl.ds(pl.multiple_of(start, COLROWS), COLROWS)]
            kinds.append(own_scalar(own, lane == 9))
            occs.append(own_scalar(own, lane == 10))
        kind = jnp.concatenate(kinds, axis=0)
        occ = jnp.concatenate(occs, axis=0)
        rows = pl.ds(pl.multiple_of(k * 64, 64), 64)
        scalar = sums[0, rows]
        vectors = [sums[m, rows] for m in (1, 2, 3)]
        weights = []
        for q in range(3):
            w = jnp.zeros((64, CHAN), jnp.float32)
            for s in range(coup_ref.shape[0]):
                w = jnp.where(kind == float(s), coup_ref[s, q : q + 1], w)
            weights.append(w)
        length = vectors[0] * vectors[0] + vectors[1] * vectors[1] + vectors[2] * vectors[2]
        product = weights[0] * scalar + weights[1] * scalar * scalar + weights[2] * length
        hidden = dot(product, head, NN, high)
        logistic = jax.nn.sigmoid(hidden)
        energy = occ * jnp.sum(ow * hidden * logistic, axis=1, keepdims=True)
        energy_ref[rows] = jnp.broadcast_to(energy, (64, CHAN))
        d_hidden = occ * ow * logistic * (1.0 + hidden * (1.0 - logistic))
        d_product = dot(d_hidden, head, NT, high)
        d_sums[0, rows] = d_product * (weights[0] + 2.0 * weights[1] * scalar)
        for m in range(3):
            d_sums[m + 1, rows] = 2.0 * weights[2] * vectors[m] * d_product
        return carry

    lax.fori_loop(0, 4, readout, 0)

    def clear(c, carry):
        rows = pl.ds(pl.multiple_of(c * RUN, RUN), RUN)
        feat_ext[rows] = jnp.zeros((RUN, CHAN), jnp.float32)
        pos_ext[rows] = jnp.zeros((RUN, CHAN), jnp.float32)
        return carry

    lax.fori_loop(0, 64, clear, 0, unroll=2)
    d_far[...] = jnp.zeros_like(d_far)
    spread = spread_ref[...].astype(jnp.bfloat16)

    def backward(k, carry):
        for s in range(2):
            back_group(
                2 * k + s, NJ_REST, REST, RUN, 0, edges, feat_win, saved, d_sums, rw_ref, spread,
                d_half.at[s], d_far.at[s], feat_ext, pos_ext,
            )
        return carry

    lax.fori_loop(0, GROUPS // 2, backward, 0)

    def gather_cell(cell, carry):
        collect(cell, ((0, zlo_ref, None), (COLROWS, mid_ref, None), (2 * COLROWS, zho_ref, None)), feat_ext, pos_ext, RUN)
        return carry

    lax.fori_loop(0, 16, gather_cell, 0)


def near_back_kernel(
    edges, feat_win, saved, d_sums, rest_mid, spread_ref, rw_ref, mid_ref, feat_ext, pos_ext, d_half, d_far
):
    feat_ext[...] = jnp.zeros_like(feat_ext)
    pos_ext[...] = jnp.zeros_like(pos_ext)
    d_far[...] = jnp.zeros_like(d_far)
    spread = spread_ref[...].astype(jnp.bfloat16)

    def backward(k, carry):
        for s in range(2):
            back_group(
                2 * k + s, NJ_NEAR, NEAR, COLROWS, COLROWS, edges, feat_win, saved, d_sums, rw_ref, spread,
                d_half.at[s], d_far.at[s], feat_ext, pos_ext,
            )
        return carry

    lax.fori_loop(0, GROUPS // 2, backward, 0)

    def gather_cell(cell, carry):
        collect(cell, ((0, mid_ref, rest_mid),), feat_ext, pos_ext, COLROWS)
        return carry

    lax.fori_loop(0, 16, gather_cell, 0)


def finish_kernel(count_ref, pos_ref, mid_ref, low_ref, high_ref, energy_ref, e_ref, f_ref, g_ref):
    lane = lax.broadcasted_iota(jnp.int32, (EXTRA, CHAN), 1)
    for cell in range(4):
        x, y = cell // 2, cell % 2
        hot = site_onehot([pos_ref[3 * cell + c] for c in range(3)], count_ref[x, 0, y]).astype(jnp.float32)
        arrived = high_ref[y] if x else low_ref[y]
        total = mid_ref[y, 1 + x] + arrived.astype(jnp.float32)
        turned = hot.T.astype(jnp.bfloat16)
        rest = total[:SLOTS]
        grad = jnp.zeros((SLOTS, CHAN), jnp.float32)
        for _ in range(3):
            piece = rest.astype(jnp.bfloat16)
            grad = grad + dot(turned, piece, NN)
            rest = rest - piece.astype(jnp.float32)
        g_ref[cell] = grad
        for c in range(3):
            force = jnp.concatenate(
                [
                    jnp.sum(jnp.where(lane == 16 * g + c, total[SLOTS:], 0.0), axis=1, keepdims=True)
                    for g in range(8)
                ],
                axis=0,
            )
            f_ref[3 * cell + c] = -jnp.sum(hot * force, axis=0, keepdims=True)
        pieces = []
        for cc in range(4):
            g = (2 * x + cc // 2) * 4 + 2 * y + cc % 2
            pieces.append(energy_ref[g * COLROWS : g * COLROWS + COLROWS, 0:1])
        e_ref[cell] = jnp.sum(hot * jnp.concatenate(pieces, axis=0), axis=0, keepdims=True)


SMEM = pl.BlockSpec(memory_space=pltpu.SMEM)
VMEM = pl.BlockSpec(memory_space=pltpu.VMEM)
HBM = pl.BlockSpec(memory_space=pltpu.HBM)


NEAR_LIMIT = 12 << 10
REST_LIMIT = 30 << 10
SORT_LIMIT = 65000


def shifted(low_part, high_part, axis):
    count = lax.axis_size(axis)
    up = [(i, (i + 1) % count) for i in range(count)]
    down = [(target, source) for source, target in up]
    from_below = lax.ppermute(high_part, axis, up)
    from_above = lax.ppermute(low_part, axis, down)
    return from_below, from_above


def call(kernel, name, outs, scratch, ins, limit, flops, spaces=()):
    shapes = tuple(jax.ShapeDtypeStruct(*out) for out in outs)
    moved = sum(int(np.prod(out.shape)) * out.dtype.itemsize for out in shapes)
    return pl.pallas_call(
        kernel,
        name=name,
        out_shape=shapes,
        in_specs=[*spaces] + [VMEM] * (len(ins) - len(spaces)),
        out_specs=(VMEM,) * len(shapes),
        scratch_shapes=[pltpu.VMEM(*one) if isinstance(one, tuple) else one for one in scratch],
        compiler_params=pltpu.CompilerParams(vmem_limit_bytes=limit << 10),
        cost_estimate=pl.CostEstimate(flops=flops, bytes_accessed=moved, transcendentals=0),
    )(*ins)


def body(local_pos, counts, species, features, radial_weights, coupling, mixing, hidden_weights, output_weights):
    bf16, f32 = jnp.bfloat16, jnp.float32
    pos = local_pos.reshape(12, 1, SLOTS)
    count = counts.transpose(0, 2, 1)
    low, high = call(
        sort_kernel,
        "sort",
        [((2, ROWS, CHAN), bf16)] * 2,
        [
            pltpu.VMEM((4, CHAN, SLOTS), f32),
            pltpu.SMEM((2, 1, 2), jnp.int32),
            pltpu.VMEM((12, 1, SLOTS), f32),
            pltpu.VMEM((4, 1, SLOTS), jnp.int32),
            pltpu.VMEM((4, SLOTS, CHAN), bf16),
            pltpu.SemaphoreType.DMA((4,)),
        ],
        (count, pos, species.reshape(4, 1, SLOTS), features.reshape(4, SLOTS, CHAN)),
        SORT_LIMIT,
        10**7,
        (HBM,) * 4,
    )
    low, high = low.reshape(2, 1, ROWS, CHAN), high.reshape(2, 1, ROWS, CHAN)
    xl, xh = shifted(low, high, "gx")
    wide = jnp.concatenate([xl, low, high, xh], axis=1)
    yl, yh = shifted(wide[:1], wide[1:], "gy")
    layer = jnp.concatenate([yl, wide, yh], axis=0)
    zl, zh = shifted(layer, layer, "gz")
    layer, zl, zh = (part.reshape(16, ROWS, CHAN) for part in (layer, zl, zh))

    near_off = jnp.asarray(offset_table(NEAR, NJ_NEAR))
    rest_off = jnp.asarray(offset_table(REST, NJ_REST))
    pick, spread = jnp.asarray(pick_table()), jnp.asarray(spread_table())
    ext = ((64 * RUN, CHAN), f32)
    near_ext = ((64 * COLROWS, CHAN), f32)
    rows = ((4, GROUPS * COLROWS, CHAN), f32)
    sums, near_win, near_edges, near_saved = call(
        near_kernel,
        "near",
        [rows, ((GROUPS, NJ_NEAR, CHAN), bf16), ((GROUPS, TERMS, NJ_NEAR), bf16), ((GROUPS, 8, COLROWS, NJ_NEAR), f32)],
        [near_ext, near_ext, ((NJ_NEAR, CHAN), bf16)],
        (layer, near_off, pick, radial_weights),
        NEAR_LIMIT,
        2 * TERMS * NJ_NEAR * CHAN * GROUPS,
    )
    z_low, z_high, rest_mid, energy, d_sums = call(
        rest_kernel,
        "rest",
        [((16, ROWS, CHAN), bf16)] * 2 + [((16, ROWS, CHAN), f32), ((GROUPS * COLROWS, CHAN), f32), rows],
        [
            ext,
            ext,
            ((GROUPS, NJ_REST, CHAN), bf16),
            ((NJ_REST, CHAN), bf16),
            ((GROUPS, TERMS, NJ_REST), bf16),
            ((GROUPS, 8, COLROWS, NJ_REST), f32),
            rows,
            ((2, TERMS, CHAN), bf16),
            ((2, 16, NJ_REST), bf16),
        ],
        (
            layer, zl, zh, sums, rest_off, pick, spread, radial_weights,
            coupling.transpose(1, 0, 2), mixing, hidden_weights.T, output_weights.reshape(1, -1),
        ),
        REST_LIMIT,
        6 * TERMS * NJ_REST * CHAN * GROUPS,
    )
    (mid,) = call(
        near_back_kernel,
        "near_back",
        [((16, ROWS, CHAN), f32)],
        [near_ext, near_ext, ((2, TERMS, CHAN), bf16), ((2, 16, NJ_NEAR), bf16)],
        (near_edges, near_win, near_saved, d_sums, rest_mid, spread, radial_weights),
        NEAR_LIMIT,
        4 * TERMS * NJ_NEAR * CHAN * GROUPS,
    )
    four = (4, 4, ROWS, CHAN)
    from_below, from_above = shifted(z_low.reshape(four), z_high.reshape(four), "gz")
    mid = mid.reshape(four)

    def summed(part):
        return mid[part] + from_below[part].astype(f32) + from_above[part].astype(f32)

    y_below, y_above = shifted(summed(slice(0, 1)).astype(bf16), summed(slice(3, 4)).astype(bf16), "gy")
    strip = summed(slice(1, 3)) + jnp.concatenate([y_below, y_above], axis=0).astype(f32)
    x_below, x_above = shifted(strip[:, :1].astype(bf16), strip[:, 3:].astype(bf16), "gx")
    atom_energy, forces, feature_grad = call(
        finish_kernel,
        "finish",
        [((4, 1, SLOTS), f32), ((12, 1, SLOTS), f32), ((4, SLOTS, CHAN), f32)],
        [],
        (count, pos, strip, x_below.reshape(2, ROWS, CHAN), x_above.reshape(2, ROWS, CHAN), energy),
        8 << 10,
        10**7,
        (SMEM,),
    )
    return (
        atom_energy.reshape(species.shape),
        forces.reshape(local_pos.shape),
        feature_grad.reshape(features.shape),
    )


def solution(mesh):
    placed = (
        P("gx", "gy", "gz", None, None),
        P("gx", "gy", "gz"),
        P("gx", "gy", "gz", None),
        P("gx", "gy", "gz", None, None),
        P(),
        P(),
        P(),
        P(),
        P(),
    )
    return jax.shard_map(
        body,
        mesh=mesh,
        in_specs=placed,
        out_specs=(
            P("gx", "gy", "gz", None),
            P("gx", "gy", "gz", None, None),
            P("gx", "gy", "gz", None, None),
        ),
        check_vma=False,
    )
```

```python
import functools

import jax
import jax.numpy as jnp
import numpy as np
from jax import lax
from jax.experimental import pallas as pl
from jax.experimental.pallas import tpu as pltpu
from jax.sharding import PartitionSpec as P

SIDE = 7.0
CUTOFF = 5.0
LAT = 4
SLOTS = LAT**3
NB = 8
CHAN = 128
EXTRA = 8
ROWS = SLOTS + EXTRA
COLROWS = 16
RUN = 3 * COLROWS
INNER = [(a, b) for a in (-1, 0, 1) for b in (-1, 0, 1)]
OUTER = [(a, b) for a in (-2, 2) for b in (-1, 0, 1)] + [(b, a) for a in (-2, 2) for b in (-1, 0, 1)]
NEAR, REST = [], []
_at = 0
for _a, _b in INNER + OUTER[:7]:
    NEAR.append((_a, _b, COLROWS, COLROWS, _at))
    _at += COLROWS
NJ_NEAR = _at
_at = 0
for _a, _b in OUTER[7:]:
    REST.append((_a, _b, COLROWS, COLROWS, _at))
    _at += COLROWS
for _first, _inner, _count in ((8, False, 8), (32, False, 8), (4, True, 12), (32, True, 12)):
    for _a, _b in INNER if _inner else OUTER:
        REST.append((_a, _b, _first, _count, _at))
        _at += _count
USED = _at
NJ_REST = 512
TILE = 128
FAR = 1000.0
GROUPS = 16
TERMS = 4 * NB * COLROWS


def offset_table(pieces, size):
    table = np.zeros((4, 8, size), np.float32)
    used = sum(piece[3] for piece in pieces)
    table[:, :3, used:] = FAR
    for parity in range(4):
        px, py = parity // 2, parity % 2
        for a, b, first, count, at in pieces:
            table[parity, 0, at : at + count] = SIDE * ((px + a) // 2)
            table[parity, 1, at : at + count] = SIDE * ((py + b) // 2)
            run = np.arange(first, first + count)
            table[parity, 2, at : at + count] = SIDE * (run // COLROWS - 1)
    return table


def pick_table():
    table = np.zeros((8, CHAN), np.float32)
    for group in range(8):
        for part in range(3):
            for comp in range(3):
                table[comp, 16 * group + 3 * part + comp] = 1.0
    return table


def constant_table():
    parts = [pick_table()]
    for pieces, size in ((NEAR, NJ_NEAR), (REST, NJ_REST)):
        table = offset_table(pieces, size).reshape(4, 8, size // TILE, TILE)
        parts.append(table.transpose(0, 2, 1, 3).reshape(-1, TILE))
    return np.concatenate(parts, axis=0)


RADIAL = 0
COUPLE = 16
NSPEC = 10
MIXING = 48
HIDDEN = 176
OUTPUT = 192
PICK = 200
NEAR_OFF = PICK + 8
REST_OFF = NEAR_OFF + 4 * 8 * (NJ_NEAR // TILE)
PACKED = REST_OFF + 4 * 8 * (NJ_REST // TILE)


def poly_coeffs():
    v = 0.5 * np.cos(np.pi * (np.arange(400) + 0.5) / 400)
    sines = np.polynomial.polynomial.polyfit(v * v, np.sin(np.pi * v) / v, 5)
    cosines = np.polynomial.polynomial.polyfit(v * v, np.cos(np.pi * v), 6)
    return [float(c) for c in sines], [float(c) for c in cosines]


SIN_C, COS_C = poly_coeffs()


def horner(coeffs, x):
    value = coeffs[-1] * x + coeffs[-2]
    for c in coeffs[-3::-1]:
        value = value * x + c
    return value


def dot(a, b, dims, precision=None):
    return lax.dot_general(a, b, (dims, ((), ())), preferred_element_type=jnp.float32, precision=precision)


def halves(x):
    first = x.astype(jnp.bfloat16)
    return first, (x - first.astype(jnp.float32)).astype(jnp.bfloat16)


def dot_parts(a, parts, dims):
    a0, a1 = halves(a)
    return dot(a0, parts[0], dims) + (dot(a0, parts[1], dims) + dot(a1, parts[0], dims))


NN = ((1,), (0,))
NT = ((1,), (1,))
TN = ((0,), (0,))


def site_onehot(pos, count):
    sx, sy, sz = (jnp.clip(jnp.floor(p * (LAT / SIDE)).astype(jnp.int32), 0, LAT - 1) for p in pos)
    row = (((sx >> 1) * 2 + (sy >> 1)) * 4 + sz) * 4 + (sx & 1) * 2 + (sy & 1)
    slot = lax.broadcasted_iota(jnp.int32, (1, SLOTS), 1)
    row = jnp.where(slot < count, row, -1)
    return lax.broadcasted_iota(jnp.int32, (SLOTS, SLOTS), 0) == row


def lane_group(rows):
    return lax.broadcasted_iota(jnp.int32, (rows, CHAN), 1) >> 4


def sort_kernel(
    count_hbm, pos_hbm, kind_hbm, feat_hbm, radial_hbm, couple_hbm, mix_hbm, hidden_hbm, output_hbm, const_hbm,
    out_ref, pack_ref, parts_ref, count_ref, pos_ref, kind_ref, feat_ref, couple_ref, output_ref, sem,
):
    copies = [
        pltpu.make_async_copy(source, target, sem.at[k])
        for k, (source, target) in enumerate(
            (
                (count_hbm, count_ref),
                (pos_hbm, pos_ref),
                (kind_hbm, kind_ref),
                (feat_hbm, feat_ref),
                (couple_hbm, couple_ref),
                (output_hbm, output_ref),
                (radial_hbm, pack_ref.at[RADIAL:COUPLE]),
                (mix_hbm, pack_ref.at[MIXING:HIDDEN]),
                (hidden_hbm, pack_ref.at[HIDDEN:OUTPUT]),
                (const_hbm, pack_ref.at[PICK:PACKED]),
            )
        )
    ]
    for copy in copies:
        copy.start()
    group = lane_group(EXTRA)
    parts_ref[...] = jnp.zeros_like(parts_ref)
    for copy in copies:
        copy.wait()
    for s in range(NSPEC):
        pack_ref[COUPLE + 3 * s : COUPLE + 3 * s + 3] = couple_ref[s]
    pack_ref[OUTPUT : OUTPUT + 1, : output_ref.shape[1]] = output_ref[...]
    for cell in range(4):
        x, y = cell // 2, cell % 2
        pos = [pos_ref[3 * cell + c] for c in range(3)]
        hot = site_onehot(pos, count_ref[x, 0, y]).astype(jnp.bfloat16)
        lines = []
        for left in pos:
            first = left.astype(jnp.bfloat16).astype(jnp.float32)
            left = left - first
            second = left.astype(jnp.bfloat16).astype(jnp.float32)
            lines.append((first, second, left - second))
        kind = kind_ref[cell].astype(jnp.float32)
        for g in range(8):
            for part in range(3):
                for c in range(3):
                    at = 16 * g + 3 * part + c
                    parts_ref[cell, at : at + 1] = lines[c][part]
            parts_ref[cell, 16 * g + 9 : 16 * g + 10] = kind
            parts_ref[cell, 16 * g + 10 : 16 * g + 11] = jnp.ones_like(kind)
        at = 2 * y + x
        out_ref[at, :SLOTS] = dot(hot, feat_ref[cell], NN).astype(jnp.bfloat16)
        spread = dot(hot, parts_ref[cell].astype(jnp.bfloat16), NT)
        extra = jnp.zeros((EXTRA, CHAN), jnp.float32)
        for g in range(8):
            extra = extra + jnp.where(group == g, spread[8 * g : 8 * g + 8], 0.0)
        out_ref[at, SLOTS:] = extra.astype(jnp.bfloat16)


def place(msg, cell, feat_ext, pos_ext, run, shift):
    group = lane_group(8)
    scalars = msg[cell, SLOTS:].astype(jnp.float32)
    for cc in range(4):
        x, y = 2 * (cell % 4) + cc // 2, 2 * (cell // 4) + cc % 2
        base = pl.multiple_of((x * 8 + y) * run + shift, COLROWS)
        feat_ext[pl.ds(base, COLROWS)] = msg[cell, COLROWS * cc : COLROWS * cc + COLROWS].astype(jnp.float32)
        for h in range(2):
            pos_ext[pl.ds(base + 8 * h, 8)] = jnp.where(group == 2 * cc + h, scalars, 0.0)


def column(g, run):
    return ((g // 4 + 2) * 8 + g % 4 + 2) * run


def own_scalar(rows, lanes):
    return jnp.sum(jnp.where(lanes, rows, 0.0), axis=1, keepdims=True)


def lane_kind():
    return lax.broadcasted_iota(jnp.int32, (COLROWS, CHAN), 1) & 15


AMP = float(np.sqrt(2.0 / CUTOFF))
ROOT3 = float(np.sqrt(3.0))


def take_window(g, pieces, run, skip, feat_ext, pos_ext, feat_win, pos_win):
    base = column(g, run)
    for a, b, first, count, at in pieces:
        start = base + (a * 8 + b) * run + first - skip
        feat_win[g, at : at + count] = feat_ext[pl.ds(start, count)].astype(jnp.bfloat16)
        pos_win[at : at + count] = pos_ext[pl.ds(start, count)].astype(jnp.bfloat16)
    own = pos_ext[pl.ds(pl.multiple_of(base + COLROWS - skip, COLROWS), COLROWS)]
    return own


def edge_columns(g, own, far, pack_ref, off_at, edges, saved, size):
    lane = lane_kind()
    coords = [own_scalar(own, (lane == c) | (lane == 3 + c) | (lane == 6 + c)) for c in range(3)]
    for t in range(size // TILE):
        at = slice(t * TILE, t * TILE + TILE)
        there = far[:, at] + pack_ref[pl.ds(pl.multiple_of(off_at + 8 * t, 8), 8)]
        dx, dy, dz = (there[c : c + 1] - coords[c] for c in range(3))
        square = dx * dx + dy * dy + dz * dz
        clear = jnp.maximum(square, 0.25)
        inv = lax.rsqrt(clear)
        u = jnp.minimum(clear * inv * (1.0 / CUTOFF), 1.0)
        inside = (square >= 0.25) & (square < CUTOFF * CUTOFF)
        v = u - 0.5
        v2 = v * v
        sine = horner(COS_C, v2)
        cosine = -(horner(SIN_C, v2) * v)
        u2 = u * u
        u4 = u2 * u2
        u5 = u4 * u
        env = 1.0 + u4 * u2 * (u * (48.0 - 21.0 * u) - 28.0)
        env = jnp.where(inside, env, 0.0)
        slope = (-168.0 / CUTOFF) * u5 * ((1.0 - u) * (1.0 - u))
        slope = jnp.where(inside, slope, 0.0) - env * inv
        ux, uy, uz = dx * inv, dy * inv, dz * inv
        for k, value in enumerate((ux, uy, uz, inv, sine, cosine, env, slope)):
            saved[g, k, :, at] = value
        yx, yy, yz = ROOT3 * ux, ROOT3 * uy, ROOT3 * uz
        twice = 2.0 * cosine
        before = jnp.zeros_like(env)
        radial = AMP * sine * inv * env
        for b in range(NB):
            r0 = b * 4 * COLROWS
            edges[g, r0 : r0 + 16, at] = radial.astype(jnp.bfloat16)
            edges[g, r0 + 16 : r0 + 32, at] = (radial * yx).astype(jnp.bfloat16)
            edges[g, r0 + 32 : r0 + 48, at] = (radial * yy).astype(jnp.bfloat16)
            edges[g, r0 + 48 : r0 + 64, at] = (radial * yz).astype(jnp.bfloat16)
            before, radial = radial, twice * radial - before


def group_rows(g):
    return pl.ds(pl.multiple_of(g * COLROWS, COLROWS), COLROWS)


def contract(g, edges, feat_win, pack_ref, sums, start_ref=None):
    summed = dot(edges[g], feat_win[g], NN)
    rows = group_rows(g)
    for m in range(4):
        total = jnp.zeros((COLROWS, CHAN), jnp.float32) if start_ref is None else start_ref[m, rows]
        for b in range(NB):
            r0 = (b * 4 + m) * COLROWS
            total = total + pack_ref[8 * min(m, 1) + b : 8 * min(m, 1) + b + 1] * summed[r0 : r0 + 16]
        sums[m, rows] = total


def back_group(g, size, pieces, run, skip, edges, feat_win, saved, d_sums, pack_ref, d_half, d_far, d_win, d_feat_ext, d_pos_ext):
    lane = lane_kind()
    base = column(g, run)
    rows = group_rows(g)
    for m in range(4):
        d_sum = d_sums[m, rows]
        for b in range(NB):
            r0 = (b * 4 + m) * COLROWS
            d_half[r0 : r0 + 16] = (pack_ref[8 * min(m, 1) + b : 8 * min(m, 1) + b + 1] * d_sum).astype(jnp.bfloat16)
    totals = [jnp.zeros((COLROWS, TILE), jnp.float32)] * 3
    for t in range(size // TILE):
        at = slice(t * TILE, t * TILE + TILE)
        d_edge = dot(d_half[...], feat_win[g, at], NT)
        ux, uy, uz, inv, sine, cosine, env, slope = (saved[g, k, :, at] for k in range(8))
        yx, yy, yz = ROOT3 * ux, ROOT3 * uy, ROOT3 * uz
        twice = 2.0 * cosine
        s_old, s_now = jnp.zeros_like(sine), sine
        c_old, c_now = jnp.ones_like(sine), cosine
        s_sum, c_sum = 0.0, 0.0
        grads = [0.0, 0.0, 0.0]
        for b in range(NB):
            r0 = b * 4 * COLROWS
            e0, e1, e2, e3 = (d_edge[r0 + 16 * m : r0 + 16 * m + 16] for m in range(4))
            w = e0 + yx * e1 + yy * e2 + yz * e3
            s_sum = s_sum + w * s_now
            c_sum = c_sum + w * (c_now * float(b + 1))
            grads = [grads[0] + e1 * s_now, grads[1] + e2 * s_now, grads[2] + e3 * s_now]
            if b + 1 < NB:
                s_old, s_now = s_now, twice * s_now - s_old
                c_old, c_now = c_now, twice * c_now - c_old
        scale = AMP * inv
        along = scale * (float(np.pi / CUTOFF) * env * c_sum + slope * s_sum)
        across = (ROOT3 * scale) * env * inv
        inner = grads[0] * ux + grads[1] * uy + grads[2] * uz
        along = along - across * inner
        ds = [along * ux + across * grads[0], along * uy + across * grads[1], along * uz + across * grads[2]]
        for c in range(3):
            totals[c] = totals[c] + ds[c]
            d_far[c : c + 1, at] = jnp.sum(ds[c], axis=0, keepdims=True)
    d_win[0] = dot(edges[g], d_half[...], TN)
    d_win[1, :, :8] = d_far[...].T
    for a, b, first, count, at in pieces:
        start = pl.ds(base + (a * 8 + b) * run + first - skip, count)
        d_feat_ext[start] = d_feat_ext[start] + d_win[0, at : at + count]
        d_pos_ext[start] = d_pos_ext[start] + d_win[1, at : at + count]
    mine = pl.ds(pl.multiple_of(base + COLROWS - skip, COLROWS), COLROWS)
    back = jnp.zeros((COLROWS, CHAN), jnp.float32)
    for c in range(3):
        back = jnp.where(lane == c, jnp.sum(totals[c], axis=1, keepdims=True), back)
    d_pos_ext[mine] = d_pos_ext[mine] - back


def collect(cell, outs, d_feat_ext, d_pos_ext, run):
    lane8 = lax.broadcasted_iota(jnp.int32, (8, CHAN), 1)
    for shift, out, more in outs:
        scalars = jnp.zeros((EXTRA, CHAN), jnp.float32)
        for cc in range(4):
            x, y = 2 * (cell % 4) + cc // 2, 2 * (cell // 4) + cc % 2
            base = pl.multiple_of((x * 8 + y) * run + shift, COLROWS)
            rows = d_feat_ext[pl.ds(base, COLROWS)]
            if more is not None:
                rows = rows + more[cell, COLROWS * cc : COLROWS * cc + COLROWS]
            out[cell, COLROWS * cc : COLROWS * cc + COLROWS] = rows.astype(out.dtype)
            for h in range(2):
                place_at = 16 * (2 * cc + h)
                block = d_pos_ext[pl.ds(base + 8 * h, 8)]
                block = jnp.where(lane8 < 6, block, 0.0)
                scalars = scalars + (pltpu.roll(block, place_at, 1) if place_at else block)
        if more is not None:
            scalars = scalars + more[cell, SLOTS:]
        out[cell, SLOTS:] = scalars.astype(out.dtype)


def near_kernel(layer_ref, pack_ref, sums, feat_win, edges, saved, feat_ext, pos_ext, pos_win):
    def spread_cell(cell, carry):
        place(layer_ref, cell, feat_ext, pos_ext, COLROWS, 0)
        return carry

    lax.fori_loop(0, 16, spread_cell, 0)
    pick = pack_ref[PICK : PICK + 8].astype(jnp.bfloat16)

    def forward(k, carry):
        for g in (4 * k, 4 * k + 1, 4 * k + 2, 4 * k + 3):
            own = take_window(g, NEAR, COLROWS, COLROWS, feat_ext, pos_ext, feat_win, pos_win)
            parity = ((g // 4) & 1) * 2 + (g & 1)
            far = dot(pick, pos_win[...], NT)
            edge_columns(g, own, far, pack_ref, NEAR_OFF + parity * (8 * NJ_NEAR // TILE), edges, saved, NJ_NEAR)
        for g in (4 * k, 4 * k + 1, 4 * k + 2, 4 * k + 3):
            contract(g, edges, feat_win, pack_ref, sums)
        return carry

    lax.fori_loop(0, GROUPS // 4, forward, 0)


def rest_kernel(
    layer_ref, zl_ref, zh_ref, near_sums, pack_ref,
    zlo_ref, zho_ref, mid_ref, d_sums,
    feat_ext, pos_ext, feat_win, pos_win, edges, saved, sums, energies, d_half, d_far, d_win,
):
    def spread_cell(cell, carry):
        place(layer_ref, cell, feat_ext, pos_ext, RUN, COLROWS)
        place(zl_ref, cell, feat_ext, pos_ext, RUN, 0)
        place(zh_ref, cell, feat_ext, pos_ext, RUN, 2 * COLROWS)
        return carry

    lax.fori_loop(0, 16, spread_cell, 0)
    pick = pack_ref[PICK : PICK + 8].astype(jnp.bfloat16)
    lane = lane_kind()
    pos_win[USED:] = jnp.zeros((NJ_REST - USED, CHAN), jnp.bfloat16)

    def forward(k, carry):
        for g in (4 * k, 4 * k + 1, 4 * k + 2, 4 * k + 3):
            own = take_window(g, REST, RUN, 0, feat_ext, pos_ext, feat_win, pos_win)
            feat_win[g, USED:] = jnp.zeros((NJ_REST - USED, CHAN), jnp.bfloat16)
            parity = ((g // 4) & 1) * 2 + (g & 1)
            far = dot(pick, pos_win[...], NT)
            edge_columns(g, own, far, pack_ref, REST_OFF + parity * (8 * NJ_REST // TILE), edges, saved, NJ_REST)
        for g in (4 * k, 4 * k + 1, 4 * k + 2, 4 * k + 3):
            contract(g, edges, feat_win, pack_ref, sums, near_sums)
        return carry

    lax.fori_loop(0, GROUPS // 4, forward, 0)

    head = dot(pack_ref[MIXING:HIDDEN], pack_ref[HIDDEN:OUTPUT], NT, lax.Precision.HIGHEST)
    head_parts = halves(head)
    ow = pack_ref[OUTPUT : OUTPUT + 1, : OUTPUT - HIDDEN]

    def readout(k, carry):
        kinds, occs = [], []
        for s in range(8):
            start = column(k * 8 + s, RUN) + COLROWS
            own = pos_ext[pl.ds(pl.multiple_of(start, COLROWS), COLROWS)]
            kinds.append(own_scalar(own, lane == 9))
            occs.append(own_scalar(own, lane == 10))
        kind = jnp.concatenate(kinds, axis=0)
        occ = jnp.concatenate(occs, axis=0)
        rows = pl.ds(pl.multiple_of(k * 128, 128), 128)
        scalar = sums[0, rows]
        vectors = [sums[m, rows] for m in (1, 2, 3)]
        weights = []
        for q in range(3):
            w = jnp.zeros((128, CHAN), jnp.float32)
            for s in range(NSPEC):
                w = jnp.where(kind == float(s), pack_ref[COUPLE + 3 * s + q : COUPLE + 3 * s + q + 1], w)
            weights.append(w)
        length = vectors[0] * vectors[0] + vectors[1] * vectors[1] + vectors[2] * vectors[2]
        product = weights[0] * scalar + weights[1] * scalar * scalar + weights[2] * length
        hidden = dot_parts(product, head_parts, NN)
        logistic = jax.nn.sigmoid(hidden)
        energy = occ * jnp.sum(ow * hidden * logistic, axis=1, keepdims=True)
        energies[rows] = jnp.broadcast_to(energy, (128, CHAN))
        d_hidden = occ * ow * logistic * (1.0 + hidden * (1.0 - logistic))
        d_product = dot_parts(d_hidden, head_parts, NT)
        d_sums[0, rows] = d_product * (weights[0] + 2.0 * weights[1] * scalar)
        for m in range(3):
            d_sums[m + 1, rows] = 2.0 * weights[2] * vectors[m] * d_product
        return carry

    lax.fori_loop(0, 2, readout, 0)

    def clear(c, carry):
        rows = pl.ds(pl.multiple_of(c * RUN, RUN), RUN)
        feat_ext[rows] = jnp.zeros((RUN, CHAN), jnp.float32)
        pos_ext[rows] = jnp.zeros((RUN, CHAN), jnp.float32)
        return carry

    lax.fori_loop(0, 64, clear, 0, unroll=2)
    for g in range(GROUPS):
        energy = energies[COLROWS * g : COLROWS * g + COLROWS]
        first = energy.astype(jnp.bfloat16).astype(jnp.float32)
        second = (energy - first).astype(jnp.bfloat16).astype(jnp.float32)
        third = energy - first - second
        mine = pl.ds(column(g, RUN) + COLROWS, COLROWS)
        pos_ext[mine] = jnp.where(
            lane == 3, first, jnp.where(lane == 4, second, jnp.where(lane == 5, third, 0.0))
        )
    d_far[...] = jnp.zeros_like(d_far)

    def backward(k, carry):
        for s in range(4):
            back_group(
                4 * k + s, NJ_REST, REST, RUN, 0, edges, feat_win, saved, d_sums, pack_ref,
                d_half.at[s], d_far.at[s], d_win.at[s], feat_ext, pos_ext,
            )
        return carry

    lax.fori_loop(0, GROUPS // 4, backward, 0)

    def gather_cell(cell, carry):
        collect(cell, ((0, zlo_ref, None), (COLROWS, mid_ref, None), (2 * COLROWS, zho_ref, None)), feat_ext, pos_ext, RUN)
        return carry

    lax.fori_loop(0, 16, gather_cell, 0)


def near_back_kernel(
    edges, feat_win, saved, d_sums, rest_mid, pack_ref, mid_ref, feat_ext, pos_ext, d_half, d_far, d_win
):
    feat_ext[...] = jnp.zeros_like(feat_ext)
    pos_ext[...] = jnp.zeros_like(pos_ext)
    d_far[...] = jnp.zeros_like(d_far)

    def backward(k, carry):
        for s in range(4):
            back_group(
                4 * k + s, NJ_NEAR, NEAR, COLROWS, COLROWS, edges, feat_win, saved, d_sums, pack_ref,
                d_half.at[s], d_far.at[s], d_win.at[s], feat_ext, pos_ext,
            )
        return carry

    lax.fori_loop(0, GROUPS // 4, backward, 0)

    def gather_cell(cell, carry):
        collect(cell, ((0, mid_ref, rest_mid),), feat_ext, pos_ext, COLROWS)
        return carry

    lax.fori_loop(0, 16, gather_cell, 0)


def finish_kernel(count_ref, pos_ref, mid_ref, arrived_ref, e_ref, f_ref, g_ref):
    lane = lax.broadcasted_iota(jnp.int32, (EXTRA, CHAN), 1)
    for cell in range(4):
        x, y = cell // 2, cell % 2
        hot = site_onehot([pos_ref[3 * cell + c] for c in range(3)], count_ref[x, 0, y]).astype(jnp.float32)
        total = mid_ref[y, x] + arrived_ref[y, x].astype(jnp.float32)
        turned = hot.T.astype(jnp.bfloat16)
        rest = total[:SLOTS]
        grad = jnp.zeros((SLOTS, CHAN), jnp.float32)
        for _ in range(3):
            piece = rest.astype(jnp.bfloat16)
            grad = grad + dot(turned, piece, NN)
            rest = rest - piece.astype(jnp.float32)
        g_ref[cell] = grad

        def per_slot(lanes):
            rows = [
                jnp.sum(jnp.where((lane >= 16 * g + lanes[0]) & (lane <= 16 * g + lanes[1]), total[SLOTS:], 0.0), axis=1, keepdims=True)
                for g in range(8)
            ]
            return jnp.sum(hot * jnp.concatenate(rows, axis=0), axis=0, keepdims=True)

        for c in range(3):
            f_ref[3 * cell + c] = -per_slot((c, c))
        e_ref[cell] = per_slot((3, 5))


SMEM = pl.BlockSpec(memory_space=pltpu.SMEM)
VMEM = pl.BlockSpec(memory_space=pltpu.VMEM)
HBM = pl.BlockSpec(memory_space=pltpu.HBM)


NEAR_LIMIT = 12 << 10
REST_LIMIT = 30 << 10
SORT_LIMIT = 65000


def moved(part, axis, step):
    count = lax.axis_size(axis)
    return lax.ppermute(part, axis, [(i, (i + step) % count) for i in range(count)])


def shifted(low_part, high_part, axis):
    return moved(high_part, axis, 1), moved(low_part, axis, -1)


def call(kernel, name, outs, scratch, ins, limit, flops, spaces=()):
    shapes = tuple(jax.ShapeDtypeStruct(*out) for out in outs)
    moved = sum(int(np.prod(out.shape)) * out.dtype.itemsize for out in shapes)
    return pl.pallas_call(
        kernel,
        name=name,
        out_shape=shapes,
        in_specs=[*spaces] + [VMEM] * (len(ins) - len(spaces)),
        out_specs=(VMEM,) * len(shapes),
        scratch_shapes=[pltpu.VMEM(*one) if isinstance(one, tuple) else one for one in scratch],
        compiler_params=pltpu.CompilerParams(vmem_limit_bytes=limit << 10),
        cost_estimate=pl.CostEstimate(flops=flops, bytes_accessed=moved, transcendentals=0),
    )(*ins)


def body(local_pos, counts, species, features, radial_weights, coupling, mixing, hidden_weights, output_weights):
    bf16, f32 = jnp.bfloat16, jnp.float32
    pos = local_pos.reshape(12, 1, SLOTS)
    count = counts.transpose(0, 2, 1)
    block, pack = call(
        sort_kernel,
        "sort",
        [((4, ROWS, CHAN), bf16), ((PACKED, CHAN), f32)],
        [
            pltpu.VMEM((4, CHAN, SLOTS), f32),
            pltpu.SMEM((2, 1, 2), jnp.int32),
            pltpu.VMEM((12, 1, SLOTS), f32),
            pltpu.VMEM((4, 1, SLOTS), jnp.int32),
            pltpu.VMEM((4, SLOTS, CHAN), bf16),
            pltpu.VMEM((NSPEC, 3, CHAN), f32),
            pltpu.VMEM((1, output_weights.shape[0]), f32),
            pltpu.SemaphoreType.DMA((10,)),
        ],
        (
            count,
            pos,
            species.reshape(4, 1, SLOTS),
            features.reshape(4, SLOTS, CHAN),
            radial_weights.reshape(2 * NB, CHAN),
            coupling.transpose(1, 0, 2),
            mixing,
            hidden_weights.T,
            output_weights.reshape(1, -1),
            jnp.asarray(constant_table()),
        ),
        SORT_LIMIT,
        10**7,
        (HBM,) * 10,
    )
    block = block.reshape(2, 2, ROWS, CHAN)
    wide = jnp.concatenate([block, moved(block, "gx", -1)], axis=1)
    layer = jnp.concatenate([wide, moved(wide, "gy", -1)], axis=0)
    zl, zh = shifted(layer, layer, "gz")
    layer, zl, zh = (part.reshape(16, ROWS, CHAN) for part in (layer, zl, zh))

    ext = ((64 * RUN, CHAN), f32)
    near_ext = ((64 * COLROWS, CHAN), f32)
    rows = ((4, GROUPS * COLROWS, CHAN), f32)
    sums, near_win, near_edges, near_saved = call(
        near_kernel,
        "near",
        [rows, ((GROUPS, NJ_NEAR, CHAN), bf16), ((GROUPS, TERMS, NJ_NEAR), bf16), ((GROUPS, 8, COLROWS, NJ_NEAR), f32)],
        [near_ext, near_ext, ((NJ_NEAR, CHAN), bf16)],
        (layer, pack),
        NEAR_LIMIT,
        2 * TERMS * NJ_NEAR * CHAN * GROUPS,
    )
    z_low, z_high, rest_mid, d_sums = call(
        rest_kernel,
        "rest",
        [((16, ROWS, CHAN), bf16)] * 2 + [((16, ROWS, CHAN), f32), rows],
        [
            ext,
            ext,
            ((GROUPS, NJ_REST, CHAN), bf16),
            ((NJ_REST, CHAN), bf16),
            ((GROUPS, TERMS, NJ_REST), bf16),
            ((GROUPS, 8, COLROWS, NJ_REST), f32),
            rows,
            ((GROUPS * COLROWS, CHAN), f32),
            ((4, TERMS, CHAN), bf16),
            ((4, 8, NJ_REST), f32),
            ((4, 2, NJ_REST, CHAN), f32),
        ],
        (
            layer, zl, zh, sums, pack,
        ),
        REST_LIMIT,
        6 * TERMS * NJ_REST * CHAN * GROUPS,
    )
    (mid,) = call(
        near_back_kernel,
        "near_back",
        [((16, ROWS, CHAN), f32)],
        [near_ext, near_ext, ((4, TERMS, CHAN), bf16), ((4, 8, NJ_NEAR), f32), ((4, 2, NJ_NEAR, CHAN), f32)],
        (near_edges, near_win, near_saved, d_sums, rest_mid, pack),
        NEAR_LIMIT,
        4 * TERMS * NJ_NEAR * CHAN * GROUPS,
    )
    four = (4, 4, ROWS, CHAN)
    from_below, from_above = shifted(z_low.reshape(four), z_high.reshape(four), "gz")
    mid = mid.reshape(four)

    def summed(part):
        return mid[part] + from_below[part].astype(f32) + from_above[part].astype(f32)

    strip = summed(slice(0, 2)) + moved(summed(slice(2, 4)).astype(bf16), "gy", 1).astype(f32)
    arrived = moved(strip[:, 2:].astype(bf16), "gx", 1)
    atom_energy, forces, feature_grad = call(
        finish_kernel,
        "finish",
        [((4, 1, SLOTS), f32), ((12, 1, SLOTS), f32), ((4, SLOTS, CHAN), f32)],
        [],
        (count, pos, strip, arrived),
        8 << 10,
        10**7,
        (SMEM,),
    )
    return (
        atom_energy.reshape(species.shape),
        forces.reshape(local_pos.shape),
        feature_grad.reshape(features.shape),
    )


def solution(mesh):
    placed = (
        P("gx", "gy", "gz", None, None),
        P("gx", "gy", "gz"),
        P("gx", "gy", "gz", None),
        P("gx", "gy", "gz", None, None),
        P(),
        P(),
        P(),
        P(),
        P(),
    )
    return jax.shard_map(
        body,
        mesh=mesh,
        in_specs=placed,
        out_specs=(
            P("gx", "gy", "gz", None),
            P("gx", "gy", "gz", None, None),
            P("gx", "gy", "gz", None, None),
        ),
        check_vma=False,
    )
```

```python
import functools

import jax
import jax.numpy as jnp
import numpy as np
from jax import lax
from jax.experimental import pallas as pl
from jax.experimental.pallas import tpu as pltpu
from jax.sharding import PartitionSpec as P

SIDE = 7.0
CUTOFF = 5.0
LAT = 4
SLOTS = LAT**3
NB = 8
CHAN = 128
EXTRA = 8
ROWS = SLOTS + EXTRA
COLROWS = 16
RUN = 3 * COLROWS
INNER = [(a, b) for a in (-1, 0, 1) for b in (-1, 0, 1)]
OUTER = [(a, b) for a in (-2, 2) for b in (-1, 0, 1)] + [(b, a) for a in (-2, 2) for b in (-1, 0, 1)]
NEAR, REST = [], []
_at = 0
for _a, _b in INNER + OUTER[:7]:
    NEAR.append((_a, _b, COLROWS, COLROWS, _at))
    _at += COLROWS
NJ_NEAR = _at
_at = 0
for _a, _b in OUTER[7:]:
    REST.append((_a, _b, COLROWS, COLROWS, _at))
    _at += COLROWS
for _first, _inner, _count in ((8, False, 8), (32, False, 8), (4, True, 12), (32, True, 12)):
    for _a, _b in INNER if _inner else OUTER:
        REST.append((_a, _b, _first, _count, _at))
        _at += _count
USED = _at
NJ_REST = 512
TILE = 128
FAR = 1000.0
GROUPS = 16
TERMS = 4 * NB * COLROWS


def offset_table(pieces, size):
    table = np.zeros((4, 8, size), np.float32)
    used = sum(piece[3] for piece in pieces)
    table[:, :3, used:] = FAR
    for parity in range(4):
        px, py = parity // 2, parity % 2
        for a, b, first, count, at in pieces:
            table[parity, 0, at : at + count] = SIDE * ((px + a) // 2)
            table[parity, 1, at : at + count] = SIDE * ((py + b) // 2)
            run = np.arange(first, first + count)
            table[parity, 2, at : at + count] = SIDE * (run // COLROWS - 1)
    return table


def pick_table():
    table = np.zeros((8, CHAN), np.float32)
    for group in range(8):
        for part in range(3):
            for comp in range(3):
                table[comp, 16 * group + 3 * part + comp] = 1.0
    return table


def constant_table():
    parts = [pick_table()]
    for pieces, size in ((NEAR, NJ_NEAR), (REST, NJ_REST)):
        table = offset_table(pieces, size).reshape(4, 8, size // TILE, TILE)
        parts.append(table.transpose(0, 2, 1, 3).reshape(-1, TILE))
    return np.concatenate(parts, axis=0)


RADIAL = 0
COUPLE = 16
NSPEC = 10
MIXING = 48
HIDDEN = 176
OUTPUT = 192
PICK = 200
NEAR_OFF = PICK + 8
REST_OFF = NEAR_OFF + 4 * 8 * (NJ_NEAR // TILE)
PACKED = REST_OFF + 4 * 8 * (NJ_REST // TILE)


def poly_coeffs():
    v = 0.5 * np.cos(np.pi * (np.arange(400) + 0.5) / 400)
    sines = np.polynomial.polynomial.polyfit(v * v, np.sin(np.pi * v) / v, 5)
    cosines = np.polynomial.polynomial.polyfit(v * v, np.cos(np.pi * v), 6)
    return [float(c) for c in sines], [float(c) for c in cosines]


SIN_C, COS_C = poly_coeffs()


def horner(coeffs, x):
    value = coeffs[-1] * x + coeffs[-2]
    for c in coeffs[-3::-1]:
        value = value * x + c
    return value


def dot(a, b, dims, precision=None):
    return lax.dot_general(a, b, (dims, ((), ())), preferred_element_type=jnp.float32, precision=precision)


def halves(x):
    first = x.astype(jnp.bfloat16)
    return first, (x - first.astype(jnp.float32)).astype(jnp.bfloat16)


def dot_parts(a, parts, dims):
    a0, a1 = halves(a)
    return dot(a0, parts[0], dims) + (dot(a0, parts[1], dims) + dot(a1, parts[0], dims))


NN = ((1,), (0,))
NT = ((1,), (1,))
TN = ((0,), (0,))


def site_onehot(pos, count):
    sx, sy, sz = (jnp.clip(jnp.floor(p * (LAT / SIDE)).astype(jnp.int32), 0, LAT - 1) for p in pos)
    row = (((sx >> 1) * 2 + (sy >> 1)) * 4 + sz) * 4 + (sx & 1) * 2 + (sy & 1)
    slot = lax.broadcasted_iota(jnp.int32, (1, SLOTS), 1)
    row = jnp.where(slot < count, row, -1)
    return lax.broadcasted_iota(jnp.int32, (SLOTS, SLOTS), 0) == row


def lane_group(rows):
    return lax.broadcasted_iota(jnp.int32, (rows, CHAN), 1) >> 4


def sort_kernel(
    count_hbm, pos_hbm, kind_hbm, feat_hbm, radial_hbm, couple_hbm, mix_hbm, hidden_hbm, output_hbm, const_hbm,
    out_ref, pack_ref, parts_ref, count_ref, pos_ref, kind_ref, feat_ref, couple_ref, output_ref, sem,
):
    copies = [
        pltpu.make_async_copy(source, target, sem.at[k])
        for k, (source, target) in enumerate(
            (
                (count_hbm, count_ref),
                (pos_hbm, pos_ref),
                (kind_hbm, kind_ref),
                (feat_hbm, feat_ref),
                (couple_hbm, couple_ref),
                (output_hbm, output_ref),
                (radial_hbm, pack_ref.at[RADIAL:COUPLE]),
                (mix_hbm, pack_ref.at[MIXING:HIDDEN]),
                (hidden_hbm, pack_ref.at[HIDDEN:OUTPUT]),
                (const_hbm, pack_ref.at[PICK:PACKED]),
            )
        )
    ]
    for copy in copies:
        copy.start()
    group = lane_group(EXTRA)
    parts_ref[...] = jnp.zeros_like(parts_ref)
    for copy in copies:
        copy.wait()
    for s in range(NSPEC):
        pack_ref[COUPLE + 3 * s : COUPLE + 3 * s + 3] = couple_ref[s]
    pack_ref[OUTPUT : OUTPUT + 1, : output_ref.shape[1]] = output_ref[...]
    for cell in range(4):
        x, y = cell // 2, cell % 2
        pos = [pos_ref[3 * cell + c] for c in range(3)]
        hot = site_onehot(pos, count_ref[x, 0, y]).astype(jnp.bfloat16)
        lines = []
        for left in pos:
            first = left.astype(jnp.bfloat16).astype(jnp.float32)
            left = left - first
            second = left.astype(jnp.bfloat16).astype(jnp.float32)
            lines.append((first, second, left - second))
        kind = kind_ref[cell].astype(jnp.float32)
        for g in range(8):
            for part in range(3):
                for c in range(3):
                    at = 16 * g + 3 * part + c
                    parts_ref[cell, at : at + 1] = lines[c][part]
            parts_ref[cell, 16 * g + 9 : 16 * g + 10] = kind
            parts_ref[cell, 16 * g + 10 : 16 * g + 11] = jnp.ones_like(kind)
        at = 2 * y + x
        out_ref[at, :SLOTS] = dot(hot, feat_ref[cell], NN).astype(jnp.bfloat16)
        spread = dot(hot, parts_ref[cell].astype(jnp.bfloat16), NT)
        extra = jnp.zeros((EXTRA, CHAN), jnp.float32)
        for g in range(8):
            extra = extra + jnp.where(group == g, spread[8 * g : 8 * g + 8], 0.0)
        out_ref[at, SLOTS:] = extra.astype(jnp.bfloat16)


def place(msg, cell, feat_ext, pos_ext, run, shift):
    group = lane_group(8)
    scalars = msg[cell, SLOTS:].astype(jnp.float32)
    for cc in range(4):
        x, y = 2 * (cell % 4) + cc // 2, 2 * (cell // 4) + cc % 2
        base = pl.multiple_of((x * 8 + y) * run + shift, COLROWS)
        feat_ext[pl.ds(base, COLROWS)] = msg[cell, COLROWS * cc : COLROWS * cc + COLROWS].astype(jnp.float32)
        for h in range(2):
            pos_ext[pl.ds(base + 8 * h, 8)] = jnp.where(group == 2 * cc + h, scalars, 0.0)


def column(g, run):
    return ((g // 4 + 2) * 8 + g % 4 + 2) * run


def own_scalar(rows, lanes):
    return jnp.sum(jnp.where(lanes, rows, 0.0), axis=1, keepdims=True)


def lane_kind():
    return lax.broadcasted_iota(jnp.int32, (COLROWS, CHAN), 1) & 15


AMP = float(np.sqrt(2.0 / CUTOFF))
ROOT3 = float(np.sqrt(3.0))


def take_window(g, pieces, run, skip, feat_ext, pos_ext, feat_win, pos_win):
    base = column(g, run)
    for a, b, first, count, at in pieces:
        start = base + (a * 8 + b) * run + first - skip
        feat_win[g, at : at + count] = feat_ext[pl.ds(start, count)].astype(jnp.bfloat16)
        pos_win[at : at + count] = pos_ext[pl.ds(start, count)].astype(jnp.bfloat16)
    own = pos_ext[pl.ds(pl.multiple_of(base + COLROWS - skip, COLROWS), COLROWS)]
    return own


def edge_columns(g, own, far, pack_ref, off_at, edges, saved, size):
    lane = lane_kind()
    coords = [own_scalar(own, (lane == c) | (lane == 3 + c) | (lane == 6 + c)) for c in range(3)]
    for t in range(size // TILE):
        at = slice(t * TILE, t * TILE + TILE)
        there = far[:, at] + pack_ref[pl.ds(pl.multiple_of(off_at + 8 * t, 8), 8)]
        dx, dy, dz = (there[c : c + 1] - coords[c] for c in range(3))
        square = dx * dx + dy * dy + dz * dz
        clear = jnp.maximum(square, 0.25)
        inv = lax.rsqrt(clear)
        u = jnp.minimum(clear * inv * (1.0 / CUTOFF), 1.0)
        inside = (square >= 0.25) & (square < CUTOFF * CUTOFF)
        v = u - 0.5
        v2 = v * v
        sine = horner(COS_C, v2)
        cosine = -(horner(SIN_C, v2) * v)
        u2 = u * u
        u4 = u2 * u2
        u5 = u4 * u
        env = 1.0 + u4 * u2 * (u * (48.0 - 21.0 * u) - 28.0)
        env = jnp.where(inside, env, 0.0)
        slope = (-168.0 / CUTOFF) * u5 * ((1.0 - u) * (1.0 - u))
        slope = jnp.where(inside, slope, 0.0) - env * inv
        ux, uy, uz = dx * inv, dy * inv, dz * inv
        for k, value in enumerate((ux, uy, uz, inv, sine, cosine, env, slope)):
            saved[g, k, :, at] = value
        yx, yy, yz = ROOT3 * ux, ROOT3 * uy, ROOT3 * uz
        twice = 2.0 * cosine
        before = jnp.zeros_like(env)
        radial = AMP * sine * inv * env
        for b in range(NB):
            r0 = b * 4 * COLROWS
            edges[g, r0 : r0 + 16, at] = radial.astype(jnp.bfloat16)
            edges[g, r0 + 16 : r0 + 32, at] = (radial * yx).astype(jnp.bfloat16)
            edges[g, r0 + 32 : r0 + 48, at] = (radial * yy).astype(jnp.bfloat16)
            edges[g, r0 + 48 : r0 + 64, at] = (radial * yz).astype(jnp.bfloat16)
            before, radial = radial, twice * radial - before


def group_rows(g):
    return pl.ds(pl.multiple_of(g * COLROWS, COLROWS), COLROWS)


def contract(g, edges, feat_win, pack_ref, sums, start_ref=None):
    summed = dot(edges[g], feat_win[g], NN)
    rows = group_rows(g)
    for m in range(4):
        total = jnp.zeros((COLROWS, CHAN), jnp.float32) if start_ref is None else start_ref[m, rows]
        for b in range(NB):
            r0 = (b * 4 + m) * COLROWS
            total = total + pack_ref[8 * min(m, 1) + b : 8 * min(m, 1) + b + 1] * summed[r0 : r0 + 16]
        sums[m, rows] = total


def back_group(g, size, pieces, run, skip, edges, feat_win, saved, d_sums, pack_ref, d_half, d_far, d_win, d_feat_ext, d_pos_ext):
    lane = lane_kind()
    base = column(g, run)
    rows = group_rows(g)
    for m in range(4):
        d_sum = d_sums[m, rows]
        for b in range(NB):
            r0 = (b * 4 + m) * COLROWS
            d_half[r0 : r0 + 16] = (pack_ref[8 * min(m, 1) + b : 8 * min(m, 1) + b + 1] * d_sum).astype(jnp.bfloat16)
    totals = [jnp.zeros((COLROWS, TILE), jnp.float32)] * 3
    for t in range(size // TILE):
        at = slice(t * TILE, t * TILE + TILE)
        d_edge = dot(d_half[...], feat_win[g, at], NT)
        ux, uy, uz, inv, sine, cosine, env, slope = (saved[g, k, :, at] for k in range(8))
        yx, yy, yz = ROOT3 * ux, ROOT3 * uy, ROOT3 * uz
        twice = 2.0 * cosine
        s_old, s_now = jnp.zeros_like(sine), sine
        c_old, c_now = jnp.ones_like(sine), cosine
        s_sum, c_sum = 0.0, 0.0
        grads = [0.0, 0.0, 0.0]
        for b in range(NB):
            r0 = b * 4 * COLROWS
            e0, e1, e2, e3 = (d_edge[r0 + 16 * m : r0 + 16 * m + 16] for m in range(4))
            w = e0 + yx * e1 + yy * e2 + yz * e3
            s_sum = s_sum + w * s_now
            c_sum = c_sum + w * (c_now * float(b + 1))
            grads = [grads[0] + e1 * s_now, grads[1] + e2 * s_now, grads[2] + e3 * s_now]
            if b + 1 < NB:
                s_old, s_now = s_now, twice * s_now - s_old
                c_old, c_now = c_now, twice * c_now - c_old
        scale = AMP * inv
        along = scale * (float(np.pi / CUTOFF) * env * c_sum + slope * s_sum)
        across = (ROOT3 * scale) * env * inv
        inner = grads[0] * ux + grads[1] * uy + grads[2] * uz
        along = along - across * inner
        ds = [along * ux + across * grads[0], along * uy + across * grads[1], along * uz + across * grads[2]]
        for c in range(3):
            totals[c] = totals[c] + ds[c]
            d_far[c : c + 1, at] = jnp.sum(ds[c], axis=0, keepdims=True)
    d_win[0] = dot(edges[g], d_half[...], TN)
    d_win[1, :, :8] = d_far[...].T
    for a, b, first, count, at in pieces:
        start = pl.ds(base + (a * 8 + b) * run + first - skip, count)
        d_feat_ext[start] = d_feat_ext[start] + d_win[0, at : at + count]
        d_pos_ext[start] = d_pos_ext[start] + d_win[1, at : at + count]
    mine = pl.ds(pl.multiple_of(base + COLROWS - skip, COLROWS), COLROWS)
    back = jnp.zeros((COLROWS, CHAN), jnp.float32)
    for c in range(3):
        back = jnp.where(lane == c, jnp.sum(totals[c], axis=1, keepdims=True), back)
    d_pos_ext[mine] = d_pos_ext[mine] - back


def collect(cell, outs, d_feat_ext, d_pos_ext, run):
    lane8 = lax.broadcasted_iota(jnp.int32, (8, CHAN), 1)
    for shift, out, more in outs:
        scalars = jnp.zeros((EXTRA, CHAN), jnp.float32)
        for cc in range(4):
            x, y = 2 * (cell % 4) + cc // 2, 2 * (cell // 4) + cc % 2
            base = pl.multiple_of((x * 8 + y) * run + shift, COLROWS)
            rows = d_feat_ext[pl.ds(base, COLROWS)]
            if more is not None:
                rows = rows + more[cell, COLROWS * cc : COLROWS * cc + COLROWS]
            out[cell, COLROWS * cc : COLROWS * cc + COLROWS] = rows.astype(out.dtype)
            for h in range(2):
                place_at = 16 * (2 * cc + h)
                block = d_pos_ext[pl.ds(base + 8 * h, 8)]
                block = jnp.where(lane8 < 6, block, 0.0)
                scalars = scalars + (pltpu.roll(block, place_at, 1) if place_at else block)
        if more is not None:
            scalars = scalars + more[cell, SLOTS:]
        out[cell, SLOTS:] = scalars.astype(out.dtype)


def near_kernel(layer_ref, pack_ref, sums, feat_win, edges, saved, feat_ext, pos_ext, pos_win):
    def spread_cell(cell, carry):
        place(layer_ref, cell, feat_ext, pos_ext, COLROWS, 0)
        return carry

    lax.fori_loop(0, 16, spread_cell, 0)
    pick = pack_ref[PICK : PICK + 8].astype(jnp.bfloat16)

    def forward(k, carry):
        for g in (4 * k, 4 * k + 1, 4 * k + 2, 4 * k + 3):
            own = take_window(g, NEAR, COLROWS, COLROWS, feat_ext, pos_ext, feat_win, pos_win)
            parity = ((g // 4) & 1) * 2 + (g & 1)
            far = dot(pick, pos_win[...], NT)
            edge_columns(g, own, far, pack_ref, NEAR_OFF + parity * (8 * NJ_NEAR // TILE), edges, saved, NJ_NEAR)
        for g in (4 * k, 4 * k + 1, 4 * k + 2, 4 * k + 3):
            contract(g, edges, feat_win, pack_ref, sums)
        return carry

    lax.fori_loop(0, GROUPS // 4, forward, 0)


def rest_kernel(
    layer_ref, zl_ref, zh_ref, near_sums, pack_ref,
    zlo_ref, zho_ref, mid_ref, d_sums,
    feat_ext, pos_ext, feat_win, pos_win, edges, saved, sums, energies, d_half, d_far, d_win,
):
    def spread_cell(cell, carry):
        place(layer_ref, cell, feat_ext, pos_ext, RUN, COLROWS)
        place(zl_ref, cell, feat_ext, pos_ext, RUN, 0)
        place(zh_ref, cell, feat_ext, pos_ext, RUN, 2 * COLROWS)
        return carry

    lax.fori_loop(0, 16, spread_cell, 0)
    pick = pack_ref[PICK : PICK + 8].astype(jnp.bfloat16)
    lane = lane_kind()
    pos_win[USED:] = jnp.zeros((NJ_REST - USED, CHAN), jnp.bfloat16)

    def forward(k, carry):
        for g in (4 * k, 4 * k + 1, 4 * k + 2, 4 * k + 3):
            own = take_window(g, REST, RUN, 0, feat_ext, pos_ext, feat_win, pos_win)
            feat_win[g, USED:] = jnp.zeros((NJ_REST - USED, CHAN), jnp.bfloat16)
            parity = ((g // 4) & 1) * 2 + (g & 1)
            far = dot(pick, pos_win[...], NT)
            edge_columns(g, own, far, pack_ref, REST_OFF + parity * (8 * NJ_REST // TILE), edges, saved, NJ_REST)
        for g in (4 * k, 4 * k + 1, 4 * k + 2, 4 * k + 3):
            contract(g, edges, feat_win, pack_ref, sums, near_sums)
        return carry

    lax.fori_loop(0, GROUPS // 4, forward, 0)

    head = dot(pack_ref[MIXING:HIDDEN], pack_ref[HIDDEN:OUTPUT], NT, lax.Precision.HIGHEST)
    head_parts = halves(head)
    ow = pack_ref[OUTPUT : OUTPUT + 1, : OUTPUT - HIDDEN]

    def readout(k, carry):
        kinds, occs = [], []
        for s in range(8):
            start = column(k * 8 + s, RUN) + COLROWS
            own = pos_ext[pl.ds(pl.multiple_of(start, COLROWS), COLROWS)]
            kinds.append(own_scalar(own, lane == 9))
            occs.append(own_scalar(own, lane == 10))
        kind = jnp.concatenate(kinds, axis=0)
        occ = jnp.concatenate(occs, axis=0)
        rows = pl.ds(pl.multiple_of(k * 128, 128), 128)
        scalar = sums[0, rows]
        vectors = [sums[m, rows] for m in (1, 2, 3)]
        weights = []
        for q in range(3):
            w = jnp.zeros((128, CHAN), jnp.float32)
            for s in range(NSPEC):
                w = jnp.where(kind == float(s), pack_ref[COUPLE + 3 * s + q : COUPLE + 3 * s + q + 1], w)
            weights.append(w)
        length = vectors[0] * vectors[0] + vectors[1] * vectors[1] + vectors[2] * vectors[2]
        product = weights[0] * scalar + weights[1] * scalar * scalar + weights[2] * length
        hidden = dot_parts(product, head_parts, NN)
        logistic = jax.nn.sigmoid(hidden)
        energy = occ * jnp.sum(ow * hidden * logistic, axis=1, keepdims=True)
        energies[rows] = jnp.broadcast_to(energy, (128, CHAN))
        d_hidden = occ * ow * logistic * (1.0 + hidden * (1.0 - logistic))
        d_product = dot_parts(d_hidden, head_parts, NT)
        d_sums[0, rows] = d_product * (weights[0] + 2.0 * weights[1] * scalar)
        for m in range(3):
            d_sums[m + 1, rows] = 2.0 * weights[2] * vectors[m] * d_product
        return carry

    lax.fori_loop(0, 2, readout, 0)

    def clear(c, carry):
        rows = pl.ds(pl.multiple_of(c * RUN, RUN), RUN)
        feat_ext[rows] = jnp.zeros((RUN, CHAN), jnp.float32)
        pos_ext[rows] = jnp.zeros((RUN, CHAN), jnp.float32)
        return carry

    lax.fori_loop(0, 64, clear, 0, unroll=2)
    for g in range(GROUPS):
        energy = energies[COLROWS * g : COLROWS * g + COLROWS]
        first = energy.astype(jnp.bfloat16).astype(jnp.float32)
        second = (energy - first).astype(jnp.bfloat16).astype(jnp.float32)
        third = energy - first - second
        mine = pl.ds(column(g, RUN) + COLROWS, COLROWS)
        pos_ext[mine] = jnp.where(
            lane == 3, first, jnp.where(lane == 4, second, jnp.where(lane == 5, third, 0.0))
        )
    d_far[...] = jnp.zeros_like(d_far)

    def backward(k, carry):
        for s in range(4):
            back_group(
                4 * k + s, NJ_REST, REST, RUN, 0, edges, feat_win, saved, d_sums, pack_ref,
                d_half.at[s], d_far.at[s], d_win.at[s], feat_ext, pos_ext,
            )
        return carry

    lax.fori_loop(0, GROUPS // 4, backward, 0)

    def gather_cell(cell, carry):
        collect(cell, ((0, zlo_ref, None), (COLROWS, mid_ref, None), (2 * COLROWS, zho_ref, None)), feat_ext, pos_ext, RUN)
        return carry

    lax.fori_loop(0, 16, gather_cell, 0)


def near_back_kernel(
    edges, feat_win, saved, d_sums, rest_mid, pack_ref, mid_ref, feat_ext, pos_ext, d_half, d_far, d_win
):
    feat_ext[...] = jnp.zeros_like(feat_ext)
    pos_ext[...] = jnp.zeros_like(pos_ext)
    d_far[...] = jnp.zeros_like(d_far)

    def backward(k, carry):
        for s in range(4):
            back_group(
                4 * k + s, NJ_NEAR, NEAR, COLROWS, COLROWS, edges, feat_win, saved, d_sums, pack_ref,
                d_half.at[s], d_far.at[s], d_win.at[s], feat_ext, pos_ext,
            )
        return carry

    lax.fori_loop(0, GROUPS // 4, backward, 0)

    def gather_cell(cell, carry):
        collect(cell, ((0, mid_ref, rest_mid),), feat_ext, pos_ext, COLROWS)
        return carry

    lax.fori_loop(0, 16, gather_cell, 0)


def stage_kernel(block_ref, pack_ref, block_out, pack_out):
    block_out[...] = block_ref[...]
    pack_out[...] = pack_ref[...]


def finish_kernel(count_ref, pos_ref, mid_ref, arrived_ref, e_ref, f_ref, g_ref):
    lane = lax.broadcasted_iota(jnp.int32, (EXTRA, CHAN), 1)
    for cell in range(4):
        x, y = cell // 2, cell % 2
        hot = site_onehot([pos_ref[3 * cell + c] for c in range(3)], count_ref[x, 0, y]).astype(jnp.float32)
        total = mid_ref[y, x] + arrived_ref[y, x].astype(jnp.float32)
        turned = hot.T.astype(jnp.bfloat16)
        rest = total[:SLOTS]
        grad = jnp.zeros((SLOTS, CHAN), jnp.float32)
        for _ in range(3):
            piece = rest.astype(jnp.bfloat16)
            grad = grad + dot(turned, piece, NN)
            rest = rest - piece.astype(jnp.float32)
        g_ref[cell] = grad

        def per_slot(lanes):
            rows = [
                jnp.sum(jnp.where((lane >= 16 * g + lanes[0]) & (lane <= 16 * g + lanes[1]), total[SLOTS:], 0.0), axis=1, keepdims=True)
                for g in range(8)
            ]
            return jnp.sum(hot * jnp.concatenate(rows, axis=0), axis=0, keepdims=True)

        for c in range(3):
            f_ref[3 * cell + c] = -per_slot((c, c))
        e_ref[cell] = per_slot((3, 5))


SMEM = pl.BlockSpec(memory_space=pltpu.SMEM)
VMEM = pl.BlockSpec(memory_space=pltpu.VMEM)
HBM = pl.BlockSpec(memory_space=pltpu.HBM)


NEAR_LIMIT = 12 << 10
REST_LIMIT = 30 << 10
SORT_LIMIT = 65000


def moved(part, axis, step):
    count = lax.axis_size(axis)
    return lax.ppermute(part, axis, [(i, (i + step) % count) for i in range(count)])


def shifted(low_part, high_part, axis):
    return moved(high_part, axis, 1), moved(low_part, axis, -1)


def call(kernel, name, outs, scratch, ins, limit, flops, spaces=()):
    shapes = tuple(jax.ShapeDtypeStruct(*out) for out in outs)
    moved = sum(int(np.prod(out.shape)) * out.dtype.itemsize for out in shapes)
    return pl.pallas_call(
        kernel,
        name=name,
        out_shape=shapes,
        in_specs=[*spaces] + [VMEM] * (len(ins) - len(spaces)),
        out_specs=(VMEM,) * len(shapes),
        scratch_shapes=[pltpu.VMEM(*one) if isinstance(one, tuple) else one for one in scratch],
        compiler_params=pltpu.CompilerParams(vmem_limit_bytes=limit << 10),
        cost_estimate=pl.CostEstimate(flops=flops, bytes_accessed=moved, transcendentals=0),
    )(*ins)


def body(local_pos, counts, species, features, radial_weights, coupling, mixing, hidden_weights, output_weights):
    bf16, f32 = jnp.bfloat16, jnp.float32
    pos = local_pos.reshape(12, 1, SLOTS)
    count = counts.transpose(0, 2, 1)
    block, pack = call(
        sort_kernel,
        "sort",
        [((4, ROWS, CHAN), bf16), ((PACKED, CHAN), f32)],
        [
            pltpu.VMEM((4, CHAN, SLOTS), f32),
            pltpu.SMEM((2, 1, 2), jnp.int32),
            pltpu.VMEM((12, 1, SLOTS), f32),
            pltpu.VMEM((4, 1, SLOTS), jnp.int32),
            pltpu.VMEM((4, SLOTS, CHAN), bf16),
            pltpu.VMEM((NSPEC, 3, CHAN), f32),
            pltpu.VMEM((1, output_weights.shape[0]), f32),
            pltpu.SemaphoreType.DMA((10,)),
        ],
        (
            count,
            pos,
            species.reshape(4, 1, SLOTS),
            features.reshape(4, SLOTS, CHAN),
            radial_weights.reshape(2 * NB, CHAN),
            coupling.transpose(1, 0, 2),
            mixing,
            hidden_weights.T,
            output_weights.reshape(1, -1),
            jnp.asarray(constant_table()),
        ),
        SORT_LIMIT,
        10**7,
        (HBM,) * 10,
    )
    block = block.reshape(2, 2, ROWS, CHAN)
    arrived = moved(block, "gx", -1)
    block, pack = call(
        stage_kernel,
        "stage",
        [((4, ROWS, CHAN), bf16), ((PACKED, CHAN), f32)],
        [],
        (block.reshape(4, ROWS, CHAN), pack),
        4 << 10,
        10**6,
    )
    wide = jnp.concatenate([block.reshape(2, 2, ROWS, CHAN), arrived], axis=1)
    layer = jnp.concatenate([wide, moved(wide, "gy", -1)], axis=0)
    zl, zh = shifted(layer, layer, "gz")
    layer, zl, zh = (part.reshape(16, ROWS, CHAN) for part in (layer, zl, zh))

    ext = ((64 * RUN, CHAN), f32)
    near_ext = ((64 * COLROWS, CHAN), f32)
    rows = ((4, GROUPS * COLROWS, CHAN), f32)
    sums, near_win, near_edges, near_saved = call(
        near_kernel,
        "near",
        [rows, ((GROUPS, NJ_NEAR, CHAN), bf16), ((GROUPS, TERMS, NJ_NEAR), bf16), ((GROUPS, 8, COLROWS, NJ_NEAR), f32)],
        [near_ext, near_ext, ((NJ_NEAR, CHAN), bf16)],
        (layer, pack),
        NEAR_LIMIT,
        2 * TERMS * NJ_NEAR * CHAN * GROUPS,
    )
    z_low, z_high, rest_mid, d_sums = call(
        rest_kernel,
        "rest",
        [((16, ROWS, CHAN), bf16)] * 2 + [((16, ROWS, CHAN), f32), rows],
        [
            ext,
            ext,
            ((GROUPS, NJ_REST, CHAN), bf16),
            ((NJ_REST, CHAN), bf16),
            ((GROUPS, TERMS, NJ_REST), bf16),
            ((GROUPS, 8, COLROWS, NJ_REST), f32),
            rows,
            ((GROUPS * COLROWS, CHAN), f32),
            ((4, TERMS, CHAN), bf16),
            ((4, 8, NJ_REST), f32),
            ((4, 2, NJ_REST, CHAN), f32),
        ],
        (
            layer, zl, zh, sums, pack,
        ),
        REST_LIMIT,
        6 * TERMS * NJ_REST * CHAN * GROUPS,
    )
    (mid,) = call(
        near_back_kernel,
        "near_back",
        [((16, ROWS, CHAN), f32)],
        [near_ext, near_ext, ((4, TERMS, CHAN), bf16), ((4, 8, NJ_NEAR), f32), ((4, 2, NJ_NEAR, CHAN), f32)],
        (near_edges, near_win, near_saved, d_sums, rest_mid, pack),
        NEAR_LIMIT,
        4 * TERMS * NJ_NEAR * CHAN * GROUPS,
    )
    four = (4, 4, ROWS, CHAN)
    from_below, from_above = shifted(z_low.reshape(four), z_high.reshape(four), "gz")
    mid = mid.reshape(four)

    def summed(part):
        return mid[part] + from_below[part].astype(f32) + from_above[part].astype(f32)

    strip = summed(slice(0, 2)) + moved(summed(slice(2, 4)).astype(bf16), "gy", 1).astype(f32)
    arrived = moved(strip[:, 2:].astype(bf16), "gx", 1)
    atom_energy, forces, feature_grad = call(
        finish_kernel,
        "finish",
        [((4, 1, SLOTS), f32), ((12, 1, SLOTS), f32), ((4, SLOTS, CHAN), f32)],
        [],
        (count, pos, strip, arrived),
        8 << 10,
        10**7,
        (SMEM,),
    )
    return (
        atom_energy.reshape(species.shape),
        forces.reshape(local_pos.shape),
        feature_grad.reshape(features.shape),
    )


def solution(mesh):
    placed = (
        P("gx", "gy", "gz", None, None),
        P("gx", "gy", "gz"),
        P("gx", "gy", "gz", None),
        P("gx", "gy", "gz", None, None),
        P(),
        P(),
        P(),
        P(),
        P(),
    )
    return jax.shard_map(
        body,
        mesh=mesh,
        in_specs=placed,
        out_specs=(
            P("gx", "gy", "gz", None),
            P("gx", "gy", "gz", None, None),
            P("gx", "gy", "gz", None, None),
        ),
        check_vma=False,
    )
```

```python
import functools

import jax
import jax.numpy as jnp
import numpy as np
from jax import lax
from jax.experimental import pallas as pl
from jax.experimental.pallas import tpu as pltpu
from jax.sharding import PartitionSpec as P

SIDE = 7.0
CUTOFF = 5.0
LAT = 4
SLOTS = LAT**3
NB = 8
CHAN = 128
EXTRA = 8
ROWS = SLOTS + EXTRA
COLROWS = 16
RUN = 3 * COLROWS
INNER = [(a, b) for a in (-1, 0, 1) for b in (-1, 0, 1)]
OUTER = [(a, b) for a in (-2, 2) for b in (-1, 0, 1)] + [(b, a) for a in (-2, 2) for b in (-1, 0, 1)]
NEAR, REST = [], []


def reachable(a, b):
    return {(2, 0): (0, 1), (-2, 0): (2, 3), (0, 2): (0, 2), (0, -2): (1, 3)}[
        (a if abs(a) == 2 else 0, b if abs(b) == 2 else 0)
    ]


def add_piece(pieces, a, b, first, count, stride):
    at = sum(piece[3] for piece in pieces)
    pieces.append((a, b, first, count, at, stride))


for _a, _b in INNER:
    add_piece(NEAR, _a, _b, COLROWS, COLROWS, 1)
for _a, _b in OUTER:
    for _e in reachable(_a, _b):
        add_piece(NEAR, _a, _b, COLROWS + _e, 4, 4)
for _first in (4, 32):
    for _a, _b in INNER:
        add_piece(REST, _a, _b, _first, 12, 1)
for _first in (8, 32):
    for _a, _b in OUTER:
        for _e in reachable(_a, _b):
            add_piece(REST, _a, _b, _first + _e, 2, 4)
NJ_NEAR = 256
NJ_REST = 384
TILE = 128
FAR = 1000.0
GROUPS = 16
UNROLL = 8
TERMS = 4 * NB * COLROWS


def offset_table(pieces, size):
    table = np.zeros((4, 8, size), np.float32)
    used = sum(piece[3] for piece in pieces)
    table[:, :3, used:] = FAR
    for parity in range(4):
        px, py = parity // 2, parity % 2
        for a, b, first, count, at, stride in pieces:
            table[parity, 0, at : at + count] = SIDE * ((px + a) // 2)
            table[parity, 1, at : at + count] = SIDE * ((py + b) // 2)
            run = first + stride * np.arange(count)
            table[parity, 2, at : at + count] = SIDE * (run // COLROWS - 1)
    return table


def pick_table():
    table = np.zeros((8, CHAN), np.float32)
    for group in range(8):
        for part in range(3):
            for comp in range(3):
                table[comp, 16 * group + 3 * part + comp] = 1.0
    return table


def constant_table():
    parts = [pick_table()]
    for pieces, size in ((NEAR, NJ_NEAR), (REST, NJ_REST)):
        table = offset_table(pieces, size).reshape(4, 8, size // TILE, TILE)
        parts.append(table.transpose(0, 2, 1, 3).reshape(-1, TILE))
    return np.concatenate(parts, axis=0)


RADIAL = 0
COUPLE = 16
NSPEC = 10
MIXING = 48
HIDDEN = 176
OUTPUT = 192
PICK = 200
NEAR_OFF = PICK + 8
REST_OFF = NEAR_OFF + 4 * 8 * (NJ_NEAR // TILE)
PACKED = REST_OFF + 4 * 8 * (NJ_REST // TILE)


def poly_coeffs():
    v = 0.5 * np.cos(np.pi * (np.arange(400) + 0.5) / 400)
    sines = np.polynomial.polynomial.polyfit(v * v, np.sin(np.pi * v) / v, 5)
    cosines = np.polynomial.polynomial.polyfit(v * v, np.cos(np.pi * v), 6)
    return [float(c) for c in sines], [float(c) for c in cosines]


SIN_C, COS_C = poly_coeffs()


def horner(coeffs, x):
    value = coeffs[-1] * x + coeffs[-2]
    for c in coeffs[-3::-1]:
        value = value * x + c
    return value


def dot(a, b, dims, precision=None):
    return lax.dot_general(a, b, (dims, ((), ())), preferred_element_type=jnp.float32, precision=precision)


def halves(x):
    first = x.astype(jnp.bfloat16)
    return first, (x - first.astype(jnp.float32)).astype(jnp.bfloat16)


def dot_parts(a, parts, dims):
    a0, a1 = halves(a)
    return dot(a0, parts[0], dims) + (dot(a0, parts[1], dims) + dot(a1, parts[0], dims))


NN = ((1,), (0,))
NT = ((1,), (1,))
TN = ((0,), (0,))


def site_onehot(pos, count):
    sx, sy, sz = (jnp.clip(jnp.floor(p * (LAT / SIDE)).astype(jnp.int32), 0, LAT - 1) for p in pos)
    row = (((sx >> 1) * 2 + (sy >> 1)) * 4 + sz) * 4 + (sx & 1) * 2 + (sy & 1)
    slot = lax.broadcasted_iota(jnp.int32, (1, SLOTS), 1)
    row = jnp.where(slot < count, row, -1)
    return lax.broadcasted_iota(jnp.int32, (SLOTS, SLOTS), 0) == row


def lane_group(rows):
    return lax.broadcasted_iota(jnp.int32, (rows, CHAN), 1) >> 4


def sort_kernel(
    count_hbm, pos_hbm, kind_hbm, feat_hbm, radial_hbm, couple_hbm, mix_hbm, hidden_hbm, output_hbm, const_hbm,
    out_ref, pack_ref, parts_ref, count_ref, pos_ref, kind_ref, feat_ref, couple_ref, output_ref, sem,
):
    copies = [
        pltpu.make_async_copy(source, target, sem.at[k])
        for k, (source, target) in enumerate(
            (
                (count_hbm, count_ref),
                (pos_hbm, pos_ref),
                (kind_hbm, kind_ref),
                (feat_hbm, feat_ref),
                (couple_hbm, couple_ref),
                (output_hbm, output_ref),
                (radial_hbm, pack_ref.at[RADIAL:COUPLE]),
                (mix_hbm, pack_ref.at[MIXING:HIDDEN]),
                (hidden_hbm, pack_ref.at[HIDDEN:OUTPUT]),
                (const_hbm, pack_ref.at[PICK:PACKED]),
            )
        )
    ]
    for copy in copies:
        copy.start()
    group = lane_group(EXTRA)
    parts_ref[...] = jnp.zeros_like(parts_ref)
    for copy in copies:
        copy.wait()
    for s in range(NSPEC):
        pack_ref[COUPLE + 3 * s : COUPLE + 3 * s + 3] = couple_ref[s]
    pack_ref[OUTPUT : OUTPUT + 1, : output_ref.shape[1]] = output_ref[...]
    for cell in range(4):
        x, y = cell // 2, cell % 2
        pos = [pos_ref[3 * cell + c] for c in range(3)]
        hot = site_onehot(pos, count_ref[x, 0, y]).astype(jnp.bfloat16)
        lines = []
        for left in pos:
            first = left.astype(jnp.bfloat16).astype(jnp.float32)
            left = left - first
            second = left.astype(jnp.bfloat16).astype(jnp.float32)
            lines.append((first, second, left - second))
        kind = kind_ref[cell].astype(jnp.float32)
        for g in range(8):
            for part in range(3):
                for c in range(3):
                    at = 16 * g + 3 * part + c
                    parts_ref[cell, at : at + 1] = lines[c][part]
            parts_ref[cell, 16 * g + 9 : 16 * g + 10] = kind
            parts_ref[cell, 16 * g + 10 : 16 * g + 11] = jnp.ones_like(kind)
        at = 2 * y + x
        out_ref[at, :SLOTS] = dot(hot, feat_ref[cell], NN).astype(jnp.bfloat16)
        spread = dot(hot, parts_ref[cell].astype(jnp.bfloat16), NT)
        extra = jnp.zeros((EXTRA, CHAN), jnp.float32)
        for g in range(8):
            extra = extra + jnp.where(group == g, spread[8 * g : 8 * g + 8], 0.0)
        out_ref[at, SLOTS:] = extra.astype(jnp.bfloat16)


def place(msg, cell, feat_ext, pos_ext, run, shift):
    group = lane_group(8)
    scalars = msg[cell, SLOTS:].astype(jnp.float32)
    for cc in range(4):
        x, y = 2 * (cell % 4) + cc // 2, 2 * (cell // 4) + cc % 2
        base = pl.multiple_of((x * 8 + y) * run + shift, COLROWS)
        feat_ext[pl.ds(base, COLROWS)] = msg[cell, COLROWS * cc : COLROWS * cc + COLROWS].astype(jnp.float32)
        for h in range(2):
            pos_ext[pl.ds(base + 8 * h, 8)] = jnp.where(group == 2 * cc + h, scalars, 0.0)


def column(g, run):
    return ((g // 4 + 2) * 8 + g % 4 + 2) * run


def own_scalar(rows, lanes):
    return jnp.sum(jnp.where(lanes, rows, 0.0), axis=1, keepdims=True)


def lane_kind():
    return lax.broadcasted_iota(jnp.int32, (COLROWS, CHAN), 1) & 15


AMP = float(np.sqrt(2.0 / CUTOFF))
ROOT3 = float(np.sqrt(3.0))


def piece_rows(base, piece, run, skip):
    a, b, first, count, _, stride = piece
    start = base + (a * 8 + b) * run + first - skip
    return pl.ds(start, count, stride=stride) if stride > 1 else pl.ds(start, count)


def take_window(g, pieces, run, skip, feat_ext, pos_ext, feat_win, feat_rows, pos_rows):
    base = column(g, run)
    for piece in pieces:
        rows, at, count = piece_rows(base, piece, run, skip), piece[4], piece[3]
        feat_rows[at : at + count] = feat_ext[rows]
        pos_rows[at : at + count] = pos_ext[rows]
    feat_win[g] = feat_rows[...].astype(jnp.bfloat16)
    return pos_ext[pl.ds(pl.multiple_of(base + COLROWS - skip, COLROWS), COLROWS)]


def edge_columns(g, own, far, pack_ref, off_at, edges, saved, size):
    lane = lane_kind()
    coords = [own_scalar(own, (lane == c) | (lane == 3 + c) | (lane == 6 + c)) for c in range(3)]
    for t in range(size // TILE):
        at = slice(t * TILE, t * TILE + TILE)
        there = far[:, at] + pack_ref[pl.ds(pl.multiple_of(off_at + 8 * t, 8), 8)]
        dx, dy, dz = (there[c : c + 1] - coords[c] for c in range(3))
        square = dx * dx + dy * dy + dz * dz
        clear = jnp.maximum(square, 0.25)
        inv = lax.rsqrt(clear)
        u = jnp.minimum(clear * inv * (1.0 / CUTOFF), 1.0)
        inside = (square >= 0.25) & (square < CUTOFF * CUTOFF)
        v = u - 0.5
        v2 = v * v
        sine = horner(COS_C, v2)
        cosine = -(horner(SIN_C, v2) * v)
        u2 = u * u
        u4 = u2 * u2
        u5 = u4 * u
        env = 1.0 + u4 * u2 * (u * (48.0 - 21.0 * u) - 28.0)
        env = jnp.where(inside, env, 0.0)
        slope = (-168.0 / CUTOFF) * u5 * ((1.0 - u) * (1.0 - u))
        slope = jnp.where(inside, slope, 0.0) - env * inv
        ux, uy, uz = dx * inv, dy * inv, dz * inv
        for k, value in enumerate((ux, uy, uz, inv, sine, cosine, env, slope)):
            saved[g, k, :, at] = value
        yx, yy, yz = ROOT3 * ux, ROOT3 * uy, ROOT3 * uz
        twice = 2.0 * cosine
        before = jnp.zeros_like(env)
        radial = AMP * sine * inv * env
        for b in range(NB):
            r0 = b * 4 * COLROWS
            edges[g, r0 : r0 + 16, at] = radial.astype(jnp.bfloat16)
            edges[g, r0 + 16 : r0 + 32, at] = (radial * yx).astype(jnp.bfloat16)
            edges[g, r0 + 32 : r0 + 48, at] = (radial * yy).astype(jnp.bfloat16)
            edges[g, r0 + 48 : r0 + 64, at] = (radial * yz).astype(jnp.bfloat16)
            before, radial = radial, twice * radial - before


def group_rows(g):
    return pl.ds(pl.multiple_of(g * COLROWS, COLROWS), COLROWS)


def contract(g, edges, feat_win, pack_ref, sums, start_ref=None):
    summed = dot(edges[g], feat_win[g], NN)
    rows = group_rows(g)
    for m in range(4):
        total = jnp.zeros((COLROWS, CHAN), jnp.float32) if start_ref is None else start_ref[m, rows]
        for b in range(NB):
            r0 = (b * 4 + m) * COLROWS
            total = total + pack_ref[8 * min(m, 1) + b : 8 * min(m, 1) + b + 1] * summed[r0 : r0 + 16]
        sums[m, rows] = total


def back_group(g, size, pieces, run, skip, edges, feat_win, saved, d_sums, pack_ref, d_half, d_far, d_win, d_feat_ext, d_pos_ext):
    lane = lane_kind()
    base = column(g, run)
    rows = group_rows(g)
    for m in range(4):
        d_sum = d_sums[m, rows]
        for b in range(NB):
            r0 = (b * 4 + m) * COLROWS
            d_half[r0 : r0 + 16] = (pack_ref[8 * min(m, 1) + b : 8 * min(m, 1) + b + 1] * d_sum).astype(jnp.bfloat16)
    totals = [jnp.zeros((COLROWS, TILE), jnp.float32)] * 3
    for t in range(size // TILE):
        at = slice(t * TILE, t * TILE + TILE)
        d_edge = dot(d_half[...], feat_win[g, at], NT)
        ux, uy, uz, inv, sine, cosine, env, slope = (saved[g, k, :, at] for k in range(8))
        yx, yy, yz = ROOT3 * ux, ROOT3 * uy, ROOT3 * uz
        twice = 2.0 * cosine
        s_old, s_now = jnp.zeros_like(sine), sine
        c_old, c_now = jnp.ones_like(sine), cosine
        s_sum, c_sum = 0.0, 0.0
        grads = [0.0, 0.0, 0.0]
        for b in range(NB):
            r0 = b * 4 * COLROWS
            e0, e1, e2, e3 = (d_edge[r0 + 16 * m : r0 + 16 * m + 16] for m in range(4))
            w = e0 + yx * e1 + yy * e2 + yz * e3
            s_sum = s_sum + w * s_now
            c_sum = c_sum + w * (c_now * float(b + 1))
            grads = [grads[0] + e1 * s_now, grads[1] + e2 * s_now, grads[2] + e3 * s_now]
            if b + 1 < NB:
                s_old, s_now = s_now, twice * s_now - s_old
                c_old, c_now = c_now, twice * c_now - c_old
        scale = AMP * inv
        along = scale * (float(np.pi / CUTOFF) * env * c_sum + slope * s_sum)
        across = (ROOT3 * scale) * env * inv
        inner = grads[0] * ux + grads[1] * uy + grads[2] * uz
        along = along - across * inner
        ds = [along * ux + across * grads[0], along * uy + across * grads[1], along * uz + across * grads[2]]
        for c in range(3):
            totals[c] = totals[c] + ds[c]
            d_far[c : c + 1, at] = jnp.sum(ds[c], axis=0, keepdims=True)
    d_win[0] = dot(edges[g], d_half[...], TN)
    d_win[1, :, :8] = d_far[...].T
    for piece in pieces:
        start, at, count = piece_rows(base, piece, run, skip), piece[4], piece[3]
        d_feat_ext[start] = d_feat_ext[start] + d_win[0, at : at + count]
        d_pos_ext[start] = d_pos_ext[start] + d_win[1, at : at + count]
    mine = pl.ds(pl.multiple_of(base + COLROWS - skip, COLROWS), COLROWS)
    back = jnp.zeros((COLROWS, CHAN), jnp.float32)
    for c in range(3):
        back = jnp.where(lane == c, jnp.sum(totals[c], axis=1, keepdims=True), back)
    d_pos_ext[mine] = d_pos_ext[mine] - back


def collect(cell, outs, d_feat_ext, d_pos_ext, run):
    lane8 = lax.broadcasted_iota(jnp.int32, (8, CHAN), 1)
    for shift, out, more in outs:
        scalars = jnp.zeros((EXTRA, CHAN), jnp.float32)
        for cc in range(4):
            x, y = 2 * (cell % 4) + cc // 2, 2 * (cell // 4) + cc % 2
            base = pl.multiple_of((x * 8 + y) * run + shift, COLROWS)
            rows = d_feat_ext[pl.ds(base, COLROWS)]
            if more is not None:
                rows = rows + more[cell, COLROWS * cc : COLROWS * cc + COLROWS]
            out[cell, COLROWS * cc : COLROWS * cc + COLROWS] = rows.astype(out.dtype)
            for h in range(2):
                place_at = 16 * (2 * cc + h)
                block = d_pos_ext[pl.ds(base + 8 * h, 8)]
                block = jnp.where(lane8 < 6, block, 0.0)
                scalars = scalars + (pltpu.roll(block, place_at, 1) if place_at else block)
        if more is not None:
            scalars = scalars + more[cell, SLOTS:]
        out[cell, SLOTS:] = scalars.astype(out.dtype)


def near_kernel(layer_ref, pack_ref, sums, feat_win, edges, saved, feat_ext, pos_ext, feat_rows, pos_rows):
    def spread_cell(cell, carry):
        place(layer_ref, cell, feat_ext, pos_ext, COLROWS, 0)
        return carry

    lax.fori_loop(0, 16, spread_cell, 0)
    feat_rows[...] = jnp.zeros_like(feat_rows)
    pos_rows[...] = jnp.zeros_like(pos_rows)
    pick = pack_ref[PICK : PICK + 8].astype(jnp.bfloat16)

    def forward(k, carry):
        for s in range(UNROLL):
            g = UNROLL * k + s
            own = take_window(g, NEAR, COLROWS, COLROWS, feat_ext, pos_ext, feat_win, feat_rows.at[s], pos_rows.at[s])
            parity = ((g // 4) & 1) * 2 + (g & 1)
            far = dot(pick, pos_rows[s].astype(jnp.bfloat16), NT)
            edge_columns(g, own, far, pack_ref, NEAR_OFF + parity * (8 * NJ_NEAR // TILE), edges, saved, NJ_NEAR)
        for s in range(UNROLL):
            contract(UNROLL * k + s, edges, feat_win, pack_ref, sums)
        return carry

    lax.fori_loop(0, GROUPS // UNROLL, forward, 0)


def rest_kernel(
    layer_ref, zl_ref, zh_ref, near_sums, pack_ref,
    zlo_ref, zho_ref, mid_ref, d_sums,
    feat_ext, pos_ext, feat_win, feat_rows, pos_rows, edges, saved, sums, energies, d_half, d_far, d_win,
):
    def spread_cell(cell, carry):
        place(layer_ref, cell, feat_ext, pos_ext, RUN, COLROWS)
        place(zl_ref, cell, feat_ext, pos_ext, RUN, 0)
        place(zh_ref, cell, feat_ext, pos_ext, RUN, 2 * COLROWS)
        return carry

    lax.fori_loop(0, 16, spread_cell, 0)
    feat_rows[...] = jnp.zeros_like(feat_rows)
    pos_rows[...] = jnp.zeros_like(pos_rows)
    pick = pack_ref[PICK : PICK + 8].astype(jnp.bfloat16)
    lane = lane_kind()

    def forward(k, carry):
        for s in range(UNROLL):
            g = UNROLL * k + s
            own = take_window(g, REST, RUN, 0, feat_ext, pos_ext, feat_win, feat_rows.at[s], pos_rows.at[s])
            parity = ((g // 4) & 1) * 2 + (g & 1)
            far = dot(pick, pos_rows[s].astype(jnp.bfloat16), NT)
            edge_columns(g, own, far, pack_ref, REST_OFF + parity * (8 * NJ_REST // TILE), edges, saved, NJ_REST)
        for s in range(UNROLL):
            contract(UNROLL * k + s, edges, feat_win, pack_ref, sums, near_sums)
        return carry

    lax.fori_loop(0, GROUPS // UNROLL, forward, 0)

    head = dot(pack_ref[MIXING:HIDDEN], pack_ref[HIDDEN:OUTPUT], NT, lax.Precision.HIGHEST)
    head_parts = halves(head)
    ow = pack_ref[OUTPUT : OUTPUT + 1, : OUTPUT - HIDDEN]

    def readout(k, carry):
        kinds, occs = [], []
        for s in range(8):
            start = column(k * 8 + s, RUN) + COLROWS
            own = pos_ext[pl.ds(pl.multiple_of(start, COLROWS), COLROWS)]
            kinds.append(own_scalar(own, lane == 9))
            occs.append(own_scalar(own, lane == 10))
        kind = jnp.concatenate(kinds, axis=0)
        occ = jnp.concatenate(occs, axis=0)
        rows = pl.ds(pl.multiple_of(k * 128, 128), 128)
        scalar = sums[0, rows]
        vectors = [sums[m, rows] for m in (1, 2, 3)]
        weights = []
        for q in range(3):
            w = jnp.zeros((128, CHAN), jnp.float32)
            for s in range(NSPEC):
                w = jnp.where(kind == float(s), pack_ref[COUPLE + 3 * s + q : COUPLE + 3 * s + q + 1], w)
            weights.append(w)
        length = vectors[0] * vectors[0] + vectors[1] * vectors[1] + vectors[2] * vectors[2]
        product = weights[0] * scalar + weights[1] * scalar * scalar + weights[2] * length
        hidden = dot_parts(product, head_parts, NN)
        logistic = jax.nn.sigmoid(hidden)
        energy = occ * jnp.sum(ow * hidden * logistic, axis=1, keepdims=True)
        energies[rows] = jnp.broadcast_to(energy, (128, CHAN))
        d_hidden = occ * ow * logistic * (1.0 + hidden * (1.0 - logistic))
        d_product = dot_parts(d_hidden, head_parts, NT)
        d_sums[0, rows] = d_product * (weights[0] + 2.0 * weights[1] * scalar)
        for m in range(3):
            d_sums[m + 1, rows] = 2.0 * weights[2] * vectors[m] * d_product
        return carry

    lax.fori_loop(0, 2, readout, 0)

    def clear(c, carry):
        rows = pl.ds(pl.multiple_of(c * RUN, RUN), RUN)
        feat_ext[rows] = jnp.zeros((RUN, CHAN), jnp.float32)
        pos_ext[rows] = jnp.zeros((RUN, CHAN), jnp.float32)
        return carry

    lax.fori_loop(0, 64, clear, 0, unroll=2)
    for g in range(GROUPS):
        energy = energies[COLROWS * g : COLROWS * g + COLROWS]
        first = energy.astype(jnp.bfloat16).astype(jnp.float32)
        second = (energy - first).astype(jnp.bfloat16).astype(jnp.float32)
        third = energy - first - second
        mine = pl.ds(column(g, RUN) + COLROWS, COLROWS)
        pos_ext[mine] = jnp.where(
            lane == 3, first, jnp.where(lane == 4, second, jnp.where(lane == 5, third, 0.0))
        )
    d_far[...] = jnp.zeros_like(d_far)

    def backward(k, carry):
        for s in range(UNROLL):
            back_group(
                UNROLL * k + s, NJ_REST, REST, RUN, 0, edges, feat_win, saved, d_sums, pack_ref,
                d_half.at[s], d_far.at[s], d_win.at[s], feat_ext, pos_ext,
            )
        return carry

    lax.fori_loop(0, GROUPS // UNROLL, backward, 0)

    def gather_cell(cell, carry):
        collect(cell, ((0, zlo_ref, None), (COLROWS, mid_ref, None), (2 * COLROWS, zho_ref, None)), feat_ext, pos_ext, RUN)
        return carry

    lax.fori_loop(0, 16, gather_cell, 0)


def near_back_kernel(
    edges, feat_win, saved, d_sums, rest_mid, pack_ref, mid_ref, feat_ext, pos_ext, d_half, d_far, d_win
):
    feat_ext[...] = jnp.zeros_like(feat_ext)
    pos_ext[...] = jnp.zeros_like(pos_ext)
    d_far[...] = jnp.zeros_like(d_far)

    def backward(k, carry):
        for s in range(UNROLL):
            back_group(
                UNROLL * k + s, NJ_NEAR, NEAR, COLROWS, COLROWS, edges, feat_win, saved, d_sums, pack_ref,
                d_half.at[s], d_far.at[s], d_win.at[s], feat_ext, pos_ext,
            )
        return carry

    lax.fori_loop(0, GROUPS // UNROLL, backward, 0)

    def gather_cell(cell, carry):
        collect(cell, ((0, mid_ref, rest_mid),), feat_ext, pos_ext, COLROWS)
        return carry

    lax.fori_loop(0, 16, gather_cell, 0)


def stage_kernel(block_ref, pack_ref, block_out, pack_out):
    block_out[...] = block_ref[...]
    pack_out[...] = pack_ref[...]


def finish_kernel(count_ref, pos_ref, mid_ref, arrived_ref, e_ref, f_ref, g_ref):
    lane = lax.broadcasted_iota(jnp.int32, (EXTRA, CHAN), 1)
    for cell in range(4):
        x, y = cell // 2, cell % 2
        hot = site_onehot([pos_ref[3 * cell + c] for c in range(3)], count_ref[x, 0, y]).astype(jnp.float32)
        total = mid_ref[y, x] + arrived_ref[y, x].astype(jnp.float32)
        turned = hot.T.astype(jnp.bfloat16)
        rest = total[:SLOTS]
        grad = jnp.zeros((SLOTS, CHAN), jnp.float32)
        for _ in range(3):
            piece = rest.astype(jnp.bfloat16)
            grad = grad + dot(turned, piece, NN)
            rest = rest - piece.astype(jnp.float32)
        g_ref[cell] = grad

        def per_slot(lanes):
            rows = [
                jnp.sum(jnp.where((lane >= 16 * g + lanes[0]) & (lane <= 16 * g + lanes[1]), total[SLOTS:], 0.0), axis=1, keepdims=True)
                for g in range(8)
            ]
            return jnp.sum(hot * jnp.concatenate(rows, axis=0), axis=0, keepdims=True)

        for c in range(3):
            f_ref[3 * cell + c] = -per_slot((c, c))
        e_ref[cell] = per_slot((3, 5))


SMEM = pl.BlockSpec(memory_space=pltpu.SMEM)
VMEM = pl.BlockSpec(memory_space=pltpu.VMEM)
HBM = pl.BlockSpec(memory_space=pltpu.HBM)


NEAR_LIMIT = 12 << 10
REST_LIMIT = 30 << 10
SORT_LIMIT = 65000


def moved(part, axis, step):
    count = lax.axis_size(axis)
    return lax.ppermute(part, axis, [(i, (i + step) % count) for i in range(count)])


def shifted(low_part, high_part, axis):
    return moved(high_part, axis, 1), moved(low_part, axis, -1)


def call(kernel, name, outs, scratch, ins, limit, flops, spaces=()):
    shapes = tuple(jax.ShapeDtypeStruct(*out) for out in outs)
    moved = sum(int(np.prod(out.shape)) * out.dtype.itemsize for out in shapes)
    return pl.pallas_call(
        kernel,
        name=name,
        out_shape=shapes,
        in_specs=[*spaces] + [VMEM] * (len(ins) - len(spaces)),
        out_specs=(VMEM,) * len(shapes),
        scratch_shapes=[pltpu.VMEM(*one) if isinstance(one, tuple) else one for one in scratch],
        compiler_params=pltpu.CompilerParams(vmem_limit_bytes=limit << 10),
        cost_estimate=pl.CostEstimate(flops=flops, bytes_accessed=moved, transcendentals=0),
    )(*ins)


def body(local_pos, counts, species, features, radial_weights, coupling, mixing, hidden_weights, output_weights):
    bf16, f32 = jnp.bfloat16, jnp.float32
    pos = local_pos.reshape(12, 1, SLOTS)
    count = counts.transpose(0, 2, 1)
    block, pack = call(
        sort_kernel,
        "sort",
        [((4, ROWS, CHAN), bf16), ((PACKED, CHAN), f32)],
        [
            pltpu.VMEM((4, CHAN, SLOTS), f32),
            pltpu.SMEM((2, 1, 2), jnp.int32),
            pltpu.VMEM((12, 1, SLOTS), f32),
            pltpu.VMEM((4, 1, SLOTS), jnp.int32),
            pltpu.VMEM((4, SLOTS, CHAN), bf16),
            pltpu.VMEM((NSPEC, 3, CHAN), f32),
            pltpu.VMEM((1, output_weights.shape[0]), f32),
            pltpu.SemaphoreType.DMA((10,)),
        ],
        (
            count,
            pos,
            species.reshape(4, 1, SLOTS),
            features.reshape(4, SLOTS, CHAN),
            radial_weights.reshape(2 * NB, CHAN),
            coupling.transpose(1, 0, 2),
            mixing,
            hidden_weights.T,
            output_weights.reshape(1, -1),
            jnp.asarray(constant_table()),
        ),
        SORT_LIMIT,
        10**7,
        (HBM,) * 10,
    )
    block = block.reshape(2, 2, ROWS, CHAN)
    arrived = moved(block, "gx", -1)
    block, pack = call(
        stage_kernel,
        "stage",
        [((4, ROWS, CHAN), bf16), ((PACKED, CHAN), f32)],
        [],
        (block.reshape(4, ROWS, CHAN), pack),
        4 << 10,
        10**6,
    )
    wide = jnp.concatenate([block.reshape(2, 2, ROWS, CHAN), arrived], axis=1)
    layer = jnp.concatenate([wide, moved(wide, "gy", -1)], axis=0)
    zl, zh = shifted(layer, layer, "gz")
    layer, zl, zh = (part.reshape(16, ROWS, CHAN) for part in (layer, zl, zh))

    ext = ((64 * RUN, CHAN), f32)
    near_ext = ((64 * COLROWS, CHAN), f32)
    rows = ((4, GROUPS * COLROWS, CHAN), f32)
    sums, near_win, near_edges, near_saved = call(
        near_kernel,
        "near",
        [rows, ((GROUPS, NJ_NEAR, CHAN), bf16), ((GROUPS, TERMS, NJ_NEAR), bf16), ((GROUPS, 8, COLROWS, NJ_NEAR), f32)],
        [near_ext, near_ext] + [((UNROLL, NJ_NEAR, CHAN), f32)] * 2,
        (layer, pack),
        NEAR_LIMIT,
        2 * TERMS * NJ_NEAR * CHAN * GROUPS,
    )
    z_low, z_high, rest_mid, d_sums = call(
        rest_kernel,
        "rest",
        [((16, ROWS, CHAN), bf16)] * 2 + [((16, ROWS, CHAN), f32), rows],
        [
            ext,
            ext,
            ((GROUPS, NJ_REST, CHAN), bf16),
            ((UNROLL, NJ_REST, CHAN), f32),
            ((UNROLL, NJ_REST, CHAN), f32),
            ((GROUPS, TERMS, NJ_REST), bf16),
            ((GROUPS, 8, COLROWS, NJ_REST), f32),
            rows,
            ((GROUPS * COLROWS, CHAN), f32),
            ((UNROLL, TERMS, CHAN), bf16),
            ((UNROLL, 8, NJ_REST), f32),
            ((UNROLL, 2, NJ_REST, CHAN), f32),
        ],
        (
            layer, zl, zh, sums, pack,
        ),
        REST_LIMIT,
        6 * TERMS * NJ_REST * CHAN * GROUPS,
    )
    (mid,) = call(
        near_back_kernel,
        "near_back",
        [((16, ROWS, CHAN), f32)],
        [near_ext, near_ext, ((UNROLL, TERMS, CHAN), bf16), ((UNROLL, 8, NJ_NEAR), f32), ((UNROLL, 2, NJ_NEAR, CHAN), f32)],
        (near_edges, near_win, near_saved, d_sums, rest_mid, pack),
        NEAR_LIMIT,
        4 * TERMS * NJ_NEAR * CHAN * GROUPS,
    )
    four = (4, 4, ROWS, CHAN)
    from_below, from_above = shifted(z_low.reshape(four), z_high.reshape(four), "gz")
    mid = mid.reshape(four)

    def summed(part):
        return mid[part] + from_below[part].astype(f32) + from_above[part].astype(f32)

    strip = summed(slice(0, 2)) + moved(summed(slice(2, 4)).astype(bf16), "gy", 1).astype(f32)
    arrived = moved(strip[:, 2:].astype(bf16), "gx", 1)
    atom_energy, forces, feature_grad = call(
        finish_kernel,
        "finish",
        [((4, 1, SLOTS), f32), ((12, 1, SLOTS), f32), ((4, SLOTS, CHAN), f32)],
        [],
        (count, pos, strip, arrived),
        8 << 10,
        10**7,
        (SMEM,),
    )
    return (
        atom_energy.reshape(species.shape),
        forces.reshape(local_pos.shape),
        feature_grad.reshape(features.shape),
    )


def solution(mesh):
    placed = (
        P("gx", "gy", "gz", None, None),
        P("gx", "gy", "gz"),
        P("gx", "gy", "gz", None),
        P("gx", "gy", "gz", None, None),
        P(),
        P(),
        P(),
        P(),
        P(),
    )
    return jax.shard_map(
        body,
        mesh=mesh,
        in_specs=placed,
        out_specs=(
            P("gx", "gy", "gz", None),
            P("gx", "gy", "gz", None, None),
            P("gx", "gy", "gz", None, None),
        ),
        check_vma=False,
    )
```

```python
import functools

import jax
import jax.numpy as jnp
import numpy as np
from jax import lax
from jax.experimental import pallas as pl
from jax.experimental.pallas import tpu as pltpu
from jax.sharding import PartitionSpec as P

SIDE = 7.0
CUTOFF = 5.0
LAT = 4
SLOTS = LAT**3
NB = 8
CHAN = 128
EXTRA = 8
ROWS = SLOTS + EXTRA
COLROWS = 16
RUN = 3 * COLROWS
INNER = [(a, b) for a in (-1, 0, 1) for b in (-1, 0, 1)]
OUTER = [(a, b) for a in (-2, 2) for b in (-1, 0, 1)] + [(b, a) for a in (-2, 2) for b in (-1, 0, 1)]
NEAR, REST = [], []


def reachable(a, b):
    return {(2, 0): (0, 1), (-2, 0): (2, 3), (0, 2): (0, 2), (0, -2): (1, 3)}[
        (a if abs(a) == 2 else 0, b if abs(b) == 2 else 0)
    ]


def add_piece(pieces, a, b, first, count, stride):
    at = sum(piece[3] for piece in pieces)
    pieces.append((a, b, first, count, at, stride))


for _a, _b in INNER:
    add_piece(NEAR, _a, _b, COLROWS, COLROWS, 1)
for _a, _b in OUTER:
    for _e in reachable(_a, _b):
        add_piece(NEAR, _a, _b, COLROWS + _e, 4, 4)
for _first in (4, 32):
    for _a, _b in INNER:
        add_piece(REST, _a, _b, _first, 12, 1)
for _first in (8, 32):
    for _a, _b in OUTER:
        for _e in reachable(_a, _b):
            add_piece(REST, _a, _b, _first + _e, 2, 4)
NJ_NEAR = 256
NJ_REST = 384
TILE = 128
FAR = 1000.0
GROUPS = 16
UNROLL = 8
TERMS = 4 * NB * COLROWS


def offset_table(pieces, size):
    table = np.zeros((4, 8, size), np.float32)
    used = sum(piece[3] for piece in pieces)
    table[:, :3, used:] = FAR
    for parity in range(4):
        px, py = parity // 2, parity % 2
        for a, b, first, count, at, stride in pieces:
            table[parity, 0, at : at + count] = SIDE * ((px + a) // 2)
            table[parity, 1, at : at + count] = SIDE * ((py + b) // 2)
            run = first + stride * np.arange(count)
            table[parity, 2, at : at + count] = SIDE * (run // COLROWS - 1)
    return table


def pick_table():
    table = np.zeros((8, CHAN), np.float32)
    for group in range(8):
        for part in range(3):
            for comp in range(3):
                table[comp, 16 * group + 3 * part + comp] = 1.0
    return table


def constant_table():
    parts = [pick_table()]
    for pieces, size in ((NEAR, NJ_NEAR), (REST, NJ_REST)):
        table = offset_table(pieces, size).reshape(4, 8, size // TILE, TILE)
        parts.append(table.transpose(0, 2, 1, 3).reshape(-1, TILE))
    return np.concatenate(parts, axis=0)


RADIAL = 0
COUPLE = 16
NSPEC = 10
MIXING = 48
HIDDEN = 176
OUTPUT = 192
PICK = 200
NEAR_OFF = PICK + 8
REST_OFF = NEAR_OFF + 4 * 8 * (NJ_NEAR // TILE)
PACKED = REST_OFF + 4 * 8 * (NJ_REST // TILE)


def poly_coeffs():
    v = 0.5 * np.cos(np.pi * (np.arange(400) + 0.5) / 400)
    sines = np.polynomial.polynomial.polyfit(v * v, np.sin(np.pi * v) / v, 5)
    cosines = np.polynomial.polynomial.polyfit(v * v, np.cos(np.pi * v), 6)
    return [float(c) for c in sines], [float(c) for c in cosines]


SIN_C, COS_C = poly_coeffs()


def horner(coeffs, x):
    value = coeffs[-1] * x + coeffs[-2]
    for c in coeffs[-3::-1]:
        value = value * x + c
    return value


def dot(a, b, dims, precision=None):
    return lax.dot_general(a, b, (dims, ((), ())), preferred_element_type=jnp.float32, precision=precision)


def halves(x):
    first = x.astype(jnp.bfloat16)
    return first, (x - first.astype(jnp.float32)).astype(jnp.bfloat16)


def dot_parts(a, parts, dims):
    a0, a1 = halves(a)
    return dot(a0, parts[0], dims) + (dot(a0, parts[1], dims) + dot(a1, parts[0], dims))


NN = ((1,), (0,))
NT = ((1,), (1,))
TN = ((0,), (0,))


def site_onehot(pos, count):
    sx, sy, sz = (jnp.clip(jnp.floor(p * (LAT / SIDE)).astype(jnp.int32), 0, LAT - 1) for p in pos)
    row = (((sx >> 1) * 2 + (sy >> 1)) * 4 + sz) * 4 + (sx & 1) * 2 + (sy & 1)
    slot = lax.broadcasted_iota(jnp.int32, (1, SLOTS), 1)
    row = jnp.where(slot < count, row, -1)
    return lax.broadcasted_iota(jnp.int32, (SLOTS, SLOTS), 0) == row


def lane_group(rows):
    return lax.broadcasted_iota(jnp.int32, (rows, CHAN), 1) >> 4


def sort_kernel(
    count_hbm, pos_hbm, kind_hbm, feat_hbm, radial_hbm, couple_hbm, mix_hbm, hidden_hbm, output_hbm, const_hbm,
    out_ref, pack_ref, parts_ref, count_ref, pos_ref, kind_ref, feat_ref, couple_ref, output_ref, sem,
):
    copies = [
        pltpu.make_async_copy(source, target, sem.at[k])
        for k, (source, target) in enumerate(
            (
                (count_hbm, count_ref),
                (pos_hbm, pos_ref),
                (kind_hbm, kind_ref),
                (feat_hbm, feat_ref),
                (couple_hbm, couple_ref),
                (output_hbm, output_ref),
                (radial_hbm, pack_ref.at[RADIAL:COUPLE]),
                (mix_hbm, pack_ref.at[MIXING:HIDDEN]),
                (hidden_hbm, pack_ref.at[HIDDEN:OUTPUT]),
                (const_hbm, pack_ref.at[PICK:PACKED]),
            )
        )
    ]
    for copy in copies:
        copy.start()
    group = lane_group(EXTRA)
    parts_ref[...] = jnp.zeros_like(parts_ref)
    for copy in copies:
        copy.wait()
    for s in range(NSPEC):
        pack_ref[COUPLE + 3 * s : COUPLE + 3 * s + 3] = couple_ref[s]
    pack_ref[OUTPUT : OUTPUT + 1, : output_ref.shape[1]] = output_ref[...]
    for cell in range(4):
        x, y = cell // 2, cell % 2
        pos = [pos_ref[3 * cell + c] for c in range(3)]
        hot = site_onehot(pos, count_ref[x, 0, y]).astype(jnp.bfloat16)
        lines = []
        for left in pos:
            first = left.astype(jnp.bfloat16).astype(jnp.float32)
            left = left - first
            second = left.astype(jnp.bfloat16).astype(jnp.float32)
            lines.append((first, second, left - second))
        kind = kind_ref[cell].astype(jnp.float32)
        for g in range(8):
            for part in range(3):
                for c in range(3):
                    at = 16 * g + 3 * part + c
                    parts_ref[cell, at : at + 1] = lines[c][part]
            parts_ref[cell, 16 * g + 9 : 16 * g + 10] = kind
            parts_ref[cell, 16 * g + 10 : 16 * g + 11] = jnp.ones_like(kind)
        at = 2 * y + x
        out_ref[at, :SLOTS] = dot(hot, feat_ref[cell], NN).astype(jnp.bfloat16)
        spread = dot(hot, parts_ref[cell].astype(jnp.bfloat16), NT)
        extra = jnp.zeros((EXTRA, CHAN), jnp.float32)
        for g in range(8):
            extra = extra + jnp.where(group == g, spread[8 * g : 8 * g + 8], 0.0)
        out_ref[at, SLOTS:] = extra.astype(jnp.bfloat16)


def place(msg, cell, feat_ext, pos_ext, run, shift):
    group = lane_group(8)
    scalars = msg[cell, SLOTS:].astype(jnp.float32)
    for cc in range(4):
        x, y = 2 * (cell % 4) + cc // 2, 2 * (cell // 4) + cc % 2
        base = pl.multiple_of((x * 8 + y) * run + shift, COLROWS)
        if feat_ext is not None:
            feat_ext[pl.ds(base, COLROWS)] = msg[cell, COLROWS * cc : COLROWS * cc + COLROWS].astype(jnp.float32)
        for h in range(2):
            pos_ext[pl.ds(base + 8 * h, 8)] = jnp.where(group == 2 * cc + h, scalars, 0.0)


def column(g, run):
    return ((g // 4 + 2) * 8 + g % 4 + 2) * run


def own_scalar(rows, lanes):
    return jnp.sum(jnp.where(lanes, rows, 0.0), axis=1, keepdims=True)


def lane_kind():
    return lax.broadcasted_iota(jnp.int32, (COLROWS, CHAN), 1) & 15


AMP = float(np.sqrt(2.0 / CUTOFF))
ROOT3 = float(np.sqrt(3.0))


def piece_rows(base, piece, run, skip):
    a, b, first, count, _, stride = piece
    start = base + (a * 8 + b) * run + first - skip
    return pl.ds(start, count, stride=stride) if stride > 1 else pl.ds(start, count)


def take_window(g, pieces, run, skip, feat_ext, pos_ext, feat_win, feat_rows, pos_rows):
    base = column(g, run)
    for piece in pieces:
        rows, at, count = piece_rows(base, piece, run, skip), piece[4], piece[3]
        feat_rows[at : at + count] = feat_ext[rows]
        pos_rows[at : at + count] = pos_ext[rows]
    feat_win[g] = feat_rows[...].astype(jnp.bfloat16)
    return pos_ext[pl.ds(pl.multiple_of(base + COLROWS - skip, COLROWS), COLROWS)]


def edge_columns(g, own, far, pack_ref, off_at, edges, saved, size):
    lane = lane_kind()
    coords = [own_scalar(own, (lane == c) | (lane == 3 + c) | (lane == 6 + c)) for c in range(3)]
    for t in range(size // TILE):
        at = slice(t * TILE, t * TILE + TILE)
        there = far[:, at] + pack_ref[pl.ds(pl.multiple_of(off_at + 8 * t, 8), 8)]
        dx, dy, dz = (there[c : c + 1] - coords[c] for c in range(3))
        square = dx * dx + dy * dy + dz * dz
        clear = jnp.maximum(square, 0.25)
        inv = lax.rsqrt(clear)
        u = jnp.minimum(clear * inv * (1.0 / CUTOFF), 1.0)
        inside = (square >= 0.25) & (square < CUTOFF * CUTOFF)
        v = u - 0.5
        v2 = v * v
        sine = horner(COS_C, v2)
        cosine = -(horner(SIN_C, v2) * v)
        u2 = u * u
        u4 = u2 * u2
        u5 = u4 * u
        env = 1.0 + u4 * u2 * (u * (48.0 - 21.0 * u) - 28.0)
        env = jnp.where(inside, env, 0.0)
        slope = (-168.0 / CUTOFF) * u5 * ((1.0 - u) * (1.0 - u))
        slope = jnp.where(inside, slope, 0.0) - env * inv
        ux, uy, uz = dx * inv, dy * inv, dz * inv
        for k, value in enumerate((ux, uy, uz, inv, sine, cosine, env, slope)):
            saved[g, k, :, at] = value
        yx, yy, yz = ROOT3 * ux, ROOT3 * uy, ROOT3 * uz
        twice = 2.0 * cosine
        before = jnp.zeros_like(env)
        radial = AMP * sine * inv * env
        for b in range(NB):
            r0 = b * 4 * COLROWS
            edges[g, r0 : r0 + 16, at] = radial.astype(jnp.bfloat16)
            edges[g, r0 + 16 : r0 + 32, at] = (radial * yx).astype(jnp.bfloat16)
            edges[g, r0 + 32 : r0 + 48, at] = (radial * yy).astype(jnp.bfloat16)
            edges[g, r0 + 48 : r0 + 64, at] = (radial * yz).astype(jnp.bfloat16)
            before, radial = radial, twice * radial - before


def group_rows(g):
    return pl.ds(pl.multiple_of(g * COLROWS, COLROWS), COLROWS)


def contract(g, edges, feat_win, pack_ref, sums, start_ref=None):
    summed = dot(edges[g], feat_win[g], NN)
    rows = group_rows(g)
    for m in range(4):
        total = jnp.zeros((COLROWS, CHAN), jnp.float32) if start_ref is None else start_ref[m, rows]
        for b in range(NB):
            r0 = (b * 4 + m) * COLROWS
            total = total + pack_ref[8 * min(m, 1) + b : 8 * min(m, 1) + b + 1] * summed[r0 : r0 + 16]
        sums[m, rows] = total


def back_group(g, size, pieces, run, skip, edges, feat_win, saved, d_sums, pack_ref, d_half, d_far, d_win, d_feat_ext, d_pos_ext):
    lane = lane_kind()
    base = column(g, run)
    rows = group_rows(g)
    for m in range(4):
        d_sum = d_sums[m, rows]
        for b in range(NB):
            r0 = (b * 4 + m) * COLROWS
            d_half[r0 : r0 + 16] = (pack_ref[8 * min(m, 1) + b : 8 * min(m, 1) + b + 1] * d_sum).astype(jnp.bfloat16)
    totals = [jnp.zeros((COLROWS, TILE), jnp.float32)] * 3
    for t in range(size // TILE):
        at = slice(t * TILE, t * TILE + TILE)
        d_edge = dot(d_half[...], feat_win[g, at], NT)
        ux, uy, uz, inv, sine, cosine, env, slope = (saved[g, k, :, at] for k in range(8))
        yx, yy, yz = ROOT3 * ux, ROOT3 * uy, ROOT3 * uz
        twice = 2.0 * cosine
        s_old, s_now = jnp.zeros_like(sine), sine
        c_old, c_now = jnp.ones_like(sine), cosine
        s_sum, c_sum = 0.0, 0.0
        grads = [0.0, 0.0, 0.0]
        for b in range(NB):
            r0 = b * 4 * COLROWS
            e0, e1, e2, e3 = (d_edge[r0 + 16 * m : r0 + 16 * m + 16] for m in range(4))
            w = e0 + yx * e1 + yy * e2 + yz * e3
            s_sum = s_sum + w * s_now
            c_sum = c_sum + w * (c_now * float(b + 1))
            grads = [grads[0] + e1 * s_now, grads[1] + e2 * s_now, grads[2] + e3 * s_now]
            if b + 1 < NB:
                s_old, s_now = s_now, twice * s_now - s_old
                c_old, c_now = c_now, twice * c_now - c_old
        scale = AMP * inv
        along = scale * (float(np.pi / CUTOFF) * env * c_sum + slope * s_sum)
        across = (ROOT3 * scale) * env * inv
        inner = grads[0] * ux + grads[1] * uy + grads[2] * uz
        along = along - across * inner
        ds = [along * ux + across * grads[0], along * uy + across * grads[1], along * uz + across * grads[2]]
        for c in range(3):
            totals[c] = totals[c] + ds[c]
            d_far[c : c + 1, at] = jnp.sum(ds[c], axis=0, keepdims=True)
    d_win[0] = dot(edges[g], d_half[...], TN)
    d_win[1, :, :8] = d_far[...].T
    for piece in pieces:
        start, at, count = piece_rows(base, piece, run, skip), piece[4], piece[3]
        d_feat_ext[start] = d_feat_ext[start] + d_win[0, at : at + count]
        d_pos_ext[start] = d_pos_ext[start] + d_win[1, at : at + count]
    mine = pl.ds(pl.multiple_of(base + COLROWS - skip, COLROWS), COLROWS)
    back = jnp.zeros((COLROWS, CHAN), jnp.float32)
    for c in range(3):
        back = jnp.where(lane == c, jnp.sum(totals[c], axis=1, keepdims=True), back)
    d_pos_ext[mine] = d_pos_ext[mine] - back


def collect(cell, outs, d_feat_ext, d_pos_ext, run):
    lane8 = lax.broadcasted_iota(jnp.int32, (8, CHAN), 1)
    for shift, out, more in outs:
        scalars = jnp.zeros((EXTRA, CHAN), jnp.float32)
        for cc in range(4):
            x, y = 2 * (cell % 4) + cc // 2, 2 * (cell // 4) + cc % 2
            base = pl.multiple_of((x * 8 + y) * run + shift, COLROWS)
            if out.shape[1] == ROWS:
                rows = d_feat_ext[pl.ds(base, COLROWS)]
                out[cell, COLROWS * cc : COLROWS * cc + COLROWS] = rows.astype(out.dtype)
            for h in range(2):
                place_at = 16 * (2 * cc + h)
                block = d_pos_ext[pl.ds(base + 8 * h, 8)]
                block = jnp.where(lane8 < 6, block, 0.0)
                scalars = scalars + (pltpu.roll(block, place_at, 1) if place_at else block)
        if more is not None:
            scalars = scalars + more[cell]
        out[cell, out.shape[1] - EXTRA :] = scalars.astype(out.dtype)


def near_kernel(
    layer_ref, pack_ref, sums, feat_win, edges, saved, weights_ref, head_ref,
    feat_ext, pos_ext, feat_rows, pos_rows,
):
    def spread_cell(cell, carry):
        place(layer_ref, cell, feat_ext, pos_ext, COLROWS, 0)
        return carry

    lax.fori_loop(0, 16, spread_cell, 0)
    feat_rows[...] = jnp.zeros_like(feat_rows)
    pos_rows[...] = jnp.zeros_like(pos_rows)
    pick = pack_ref[PICK : PICK + 8].astype(jnp.bfloat16)

    def forward(k, carry):
        for s in range(UNROLL):
            g = UNROLL * k + s
            own = take_window(g, NEAR, COLROWS, COLROWS, feat_ext, pos_ext, feat_win, feat_rows.at[s], pos_rows.at[s])
            parity = ((g // 4) & 1) * 2 + (g & 1)
            far = dot(pick, pos_rows[s].astype(jnp.bfloat16), NT)
            edge_columns(g, own, far, pack_ref, NEAR_OFF + parity * (8 * NJ_NEAR // TILE), edges, saved, NJ_NEAR)
        for s in range(UNROLL):
            contract(UNROLL * k + s, edges, feat_win, pack_ref, sums)
        return carry

    lax.fori_loop(0, GROUPS // UNROLL, forward, 0)

    head_ref[...] = dot(pack_ref[MIXING:HIDDEN], pack_ref[HIDDEN:OUTPUT], NT, lax.Precision.HIGHEST)
    lane = lane_kind()

    def couple(g, carry):
        own = pos_ext[pl.ds(pl.multiple_of(column(g, COLROWS), COLROWS), COLROWS)]
        kind = own_scalar(own, lane == 9)
        for q in range(3):
            w = jnp.zeros((COLROWS, CHAN), jnp.float32)
            for s in range(NSPEC):
                w = jnp.where(kind == float(s), pack_ref[COUPLE + 3 * s + q : COUPLE + 3 * s + q + 1], w)
            weights_ref[q, group_rows(g)] = w
        return carry

    lax.fori_loop(0, GROUPS, couple, 0, unroll=4)


def rest_kernel(
    layer_ref, zl_ref, zh_ref, near_sums, weights_ref, head_ref, pack_ref,
    zlo_ref, zho_ref, mid_ref, d_sums,
    feat_ext, pos_ext, feat_win, feat_rows, pos_rows, edges, saved, sums, energies, d_half, d_far, d_win,
):
    def spread_cell(cell, carry):
        place(layer_ref, cell, None, pos_ext, RUN, COLROWS)
        place(zl_ref, cell, feat_ext, pos_ext, RUN, 0)
        place(zh_ref, cell, feat_ext, pos_ext, RUN, 2 * COLROWS)
        return carry

    lax.fori_loop(0, 16, spread_cell, 0)
    feat_rows[...] = jnp.zeros_like(feat_rows)
    pos_rows[...] = jnp.zeros_like(pos_rows)
    pick = pack_ref[PICK : PICK + 8].astype(jnp.bfloat16)
    lane = lane_kind()

    def forward(k, carry):
        for s in range(UNROLL):
            g = UNROLL * k + s
            own = take_window(g, REST, RUN, 0, feat_ext, pos_ext, feat_win, feat_rows.at[s], pos_rows.at[s])
            parity = ((g // 4) & 1) * 2 + (g & 1)
            far = dot(pick, pos_rows[s].astype(jnp.bfloat16), NT)
            edge_columns(g, own, far, pack_ref, REST_OFF + parity * (8 * NJ_REST // TILE), edges, saved, NJ_REST)
        for s in range(UNROLL):
            contract(UNROLL * k + s, edges, feat_win, pack_ref, sums, near_sums)
        return carry

    lax.fori_loop(0, GROUPS // UNROLL, forward, 0)

    head_parts = halves(head_ref[...])
    ow = pack_ref[OUTPUT : OUTPUT + 1, : OUTPUT - HIDDEN]

    def readout(k, carry):
        occs = []
        for s in range(8):
            start = column(k * 8 + s, RUN) + COLROWS
            own = pos_ext[pl.ds(pl.multiple_of(start, COLROWS), COLROWS)]
            occs.append(own_scalar(own, lane == 10))
        occ = jnp.concatenate(occs, axis=0)
        rows = pl.ds(pl.multiple_of(k * 128, 128), 128)
        scalar = sums[0, rows]
        vectors = [sums[m, rows] for m in (1, 2, 3)]
        weights = [weights_ref[q, rows] for q in range(3)]
        length = vectors[0] * vectors[0] + vectors[1] * vectors[1] + vectors[2] * vectors[2]
        product = weights[0] * scalar + weights[1] * scalar * scalar + weights[2] * length
        hidden = dot_parts(product, head_parts, NN)
        logistic = jax.nn.sigmoid(hidden)
        energy = occ * jnp.sum(ow * hidden * logistic, axis=1, keepdims=True)
        energies[rows] = jnp.broadcast_to(energy, (128, CHAN))
        d_hidden = occ * ow * logistic * (1.0 + hidden * (1.0 - logistic))
        d_product = dot_parts(d_hidden, head_parts, NT)
        d_sums[0, rows] = d_product * (weights[0] + 2.0 * weights[1] * scalar)
        for m in range(3):
            d_sums[m + 1, rows] = 2.0 * weights[2] * vectors[m] * d_product
        return carry

    lax.fori_loop(0, 2, readout, 0)

    def clear(c, carry):
        rows = pl.ds(pl.multiple_of(c * RUN, RUN), RUN)
        feat_ext[rows] = jnp.zeros((RUN, CHAN), jnp.float32)
        pos_ext[rows] = jnp.zeros((RUN, CHAN), jnp.float32)
        return carry

    lax.fori_loop(0, 64, clear, 0, unroll=2)
    for g in range(GROUPS):
        energy = energies[COLROWS * g : COLROWS * g + COLROWS]
        first = energy.astype(jnp.bfloat16).astype(jnp.float32)
        second = (energy - first).astype(jnp.bfloat16).astype(jnp.float32)
        third = energy - first - second
        mine = pl.ds(column(g, RUN) + COLROWS, COLROWS)
        pos_ext[mine] = jnp.where(
            lane == 3, first, jnp.where(lane == 4, second, jnp.where(lane == 5, third, 0.0))
        )
    d_far[...] = jnp.zeros_like(d_far)

    def backward(k, carry):
        for s in range(UNROLL):
            back_group(
                UNROLL * k + s, NJ_REST, REST, RUN, 0, edges, feat_win, saved, d_sums, pack_ref,
                d_half.at[s], d_far.at[s], d_win.at[s], feat_ext, pos_ext,
            )
        return carry

    lax.fori_loop(0, GROUPS // UNROLL, backward, 0)

    def gather_cell(cell, carry):
        collect(cell, ((0, zlo_ref, None), (COLROWS, mid_ref, None), (2 * COLROWS, zho_ref, None)), feat_ext, pos_ext, RUN)
        return carry

    lax.fori_loop(0, 16, gather_cell, 0)


def near_back_kernel(
    edges, feat_win, saved, d_sums, rest_mid, pack_ref, mid_ref, feat_ext, pos_ext, d_half, d_far, d_win
):
    feat_ext[...] = jnp.zeros_like(feat_ext)
    pos_ext[...] = jnp.zeros_like(pos_ext)
    d_far[...] = jnp.zeros_like(d_far)

    def backward(k, carry):
        for s in range(UNROLL):
            back_group(
                UNROLL * k + s, NJ_NEAR, NEAR, COLROWS, COLROWS, edges, feat_win, saved, d_sums, pack_ref,
                d_half.at[s], d_far.at[s], d_win.at[s], feat_ext, pos_ext,
            )
        return carry

    lax.fori_loop(0, GROUPS // UNROLL, backward, 0)

    def gather_cell(cell, carry):
        collect(cell, ((0, mid_ref, rest_mid),), feat_ext, pos_ext, COLROWS)
        return carry

    lax.fori_loop(0, 16, gather_cell, 0)


def stage_kernel(block_ref, pack_ref, block_out, pack_out):
    block_out[...] = block_ref[...]
    pack_out[...] = pack_ref[...]


def finish_kernel(count_ref, pos_ref, mid_ref, arrived_ref, e_ref, f_ref, g_ref):
    lane = lax.broadcasted_iota(jnp.int32, (EXTRA, CHAN), 1)
    for cell in range(4):
        x, y = cell // 2, cell % 2
        hot = site_onehot([pos_ref[3 * cell + c] for c in range(3)], count_ref[x, 0, y]).astype(jnp.float32)
        total = mid_ref[y, x] + arrived_ref[y, x].astype(jnp.float32)
        turned = hot.T.astype(jnp.bfloat16)
        rest = total[:SLOTS]
        grad = jnp.zeros((SLOTS, CHAN), jnp.float32)
        for _ in range(3):
            piece = rest.astype(jnp.bfloat16)
            grad = grad + dot(turned, piece, NN)
            rest = rest - piece.astype(jnp.float32)
        g_ref[cell] = grad

        def per_slot(lanes):
            rows = [
                jnp.sum(jnp.where((lane >= 16 * g + lanes[0]) & (lane <= 16 * g + lanes[1]), total[SLOTS:], 0.0), axis=1, keepdims=True)
                for g in range(8)
            ]
            return jnp.sum(hot * jnp.concatenate(rows, axis=0), axis=0, keepdims=True)

        for c in range(3):
            f_ref[3 * cell + c] = -per_slot((c, c))
        e_ref[cell] = per_slot((3, 5))


SMEM = pl.BlockSpec(memory_space=pltpu.SMEM)
VMEM = pl.BlockSpec(memory_space=pltpu.VMEM)
HBM = pl.BlockSpec(memory_space=pltpu.HBM)


NEAR_LIMIT = 12 << 10
REST_LIMIT = 30 << 10
SORT_LIMIT = 65000


def moved(part, axis, step):
    count = lax.axis_size(axis)
    return lax.ppermute(part, axis, [(i, (i + step) % count) for i in range(count)])


def shifted(low_part, high_part, axis):
    return moved(high_part, axis, 1), moved(low_part, axis, -1)


def call(kernel, name, outs, scratch, ins, limit, flops, spaces=()):
    shapes = tuple(jax.ShapeDtypeStruct(*out) for out in outs)
    moved = sum(int(np.prod(out.shape)) * out.dtype.itemsize for out in shapes)
    return pl.pallas_call(
        kernel,
        name=name,
        out_shape=shapes,
        in_specs=[*spaces] + [VMEM] * (len(ins) - len(spaces)),
        out_specs=(VMEM,) * len(shapes),
        scratch_shapes=[pltpu.VMEM(*one) if isinstance(one, tuple) else one for one in scratch],
        compiler_params=pltpu.CompilerParams(vmem_limit_bytes=limit << 10),
        cost_estimate=pl.CostEstimate(flops=flops, bytes_accessed=moved, transcendentals=0),
    )(*ins)


def body(local_pos, counts, species, features, radial_weights, coupling, mixing, hidden_weights, output_weights):
    bf16, f32 = jnp.bfloat16, jnp.float32
    pos = local_pos.reshape(12, 1, SLOTS)
    count = counts.transpose(0, 2, 1)
    block, pack = call(
        sort_kernel,
        "sort",
        [((4, ROWS, CHAN), bf16), ((PACKED, CHAN), f32)],
        [
            pltpu.VMEM((4, CHAN, SLOTS), f32),
            pltpu.SMEM((2, 1, 2), jnp.int32),
            pltpu.VMEM((12, 1, SLOTS), f32),
            pltpu.VMEM((4, 1, SLOTS), jnp.int32),
            pltpu.VMEM((4, SLOTS, CHAN), bf16),
            pltpu.VMEM((NSPEC, 3, CHAN), f32),
            pltpu.VMEM((1, output_weights.shape[0]), f32),
            pltpu.SemaphoreType.DMA((10,)),
        ],
        (
            count,
            pos,
            species.reshape(4, 1, SLOTS),
            features.reshape(4, SLOTS, CHAN),
            radial_weights.reshape(2 * NB, CHAN),
            coupling.transpose(1, 0, 2),
            mixing,
            hidden_weights.T,
            output_weights.reshape(1, -1),
            jnp.asarray(constant_table()),
        ),
        SORT_LIMIT,
        10**7,
        (HBM,) * 10,
    )
    block = block.reshape(2, 2, ROWS, CHAN)
    arrived = moved(block, "gx", -1)
    block, pack = call(
        stage_kernel,
        "stage",
        [((4, ROWS, CHAN), bf16), ((PACKED, CHAN), f32)],
        [],
        (block.reshape(4, ROWS, CHAN), pack),
        4 << 10,
        10**6,
    )
    wide = jnp.concatenate([block.reshape(2, 2, ROWS, CHAN), arrived], axis=1)
    layer = jnp.concatenate([wide, moved(wide, "gy", -1)], axis=0)
    zl, zh = shifted(layer, layer, "gz")
    layer, zl, zh = (part.reshape(16, ROWS, CHAN) for part in (layer, zl, zh))

    ext = ((64 * RUN, CHAN), f32)
    near_ext = ((64 * COLROWS, CHAN), f32)
    rows = ((4, GROUPS * COLROWS, CHAN), f32)
    sums, near_win, near_edges, near_saved, weights, head = call(
        near_kernel,
        "near",
        [rows, ((GROUPS, NJ_NEAR, CHAN), bf16), ((GROUPS, TERMS, NJ_NEAR), bf16), ((GROUPS, 8, COLROWS, NJ_NEAR), f32), ((3, GROUPS * COLROWS, CHAN), f32), ((CHAN, OUTPUT - HIDDEN), f32)],
        [near_ext, near_ext] + [((UNROLL, NJ_NEAR, CHAN), f32)] * 2,
        (layer, pack),
        NEAR_LIMIT,
        2 * TERMS * NJ_NEAR * CHAN * GROUPS,
    )
    z_low, z_high, rest_mid, d_sums = call(
        rest_kernel,
        "rest",
        [((16, ROWS, CHAN), bf16)] * 2 + [((16, EXTRA, CHAN), f32), rows],
        [
            ext,
            ext,
            ((GROUPS, NJ_REST, CHAN), bf16),
            ((UNROLL, NJ_REST, CHAN), f32),
            ((UNROLL, NJ_REST, CHAN), f32),
            ((GROUPS, TERMS, NJ_REST), bf16),
            ((GROUPS, 8, COLROWS, NJ_REST), f32),
            rows,
            ((GROUPS * COLROWS, CHAN), f32),
            ((UNROLL, TERMS, CHAN), bf16),
            ((UNROLL, 8, NJ_REST), f32),
            ((UNROLL, 2, NJ_REST, CHAN), f32),
        ],
        (
            layer, zl, zh, sums, weights, head, pack,
        ),
        REST_LIMIT,
        6 * TERMS * NJ_REST * CHAN * GROUPS,
    )
    (mid,) = call(
        near_back_kernel,
        "near_back",
        [((16, ROWS, CHAN), f32)],
        [near_ext, near_ext, ((UNROLL, TERMS, CHAN), bf16), ((UNROLL, 8, NJ_NEAR), f32), ((UNROLL, 2, NJ_NEAR, CHAN), f32)],
        (near_edges, near_win, near_saved, d_sums, rest_mid, pack),
        NEAR_LIMIT,
        4 * TERMS * NJ_NEAR * CHAN * GROUPS,
    )
    four = (4, 4, ROWS, CHAN)
    from_below, from_above = shifted(z_low.reshape(four), z_high.reshape(four), "gz")
    mid = mid.reshape(four)

    def summed(part):
        return mid[part] + from_below[part].astype(f32) + from_above[part].astype(f32)

    strip = summed(slice(0, 2)) + moved(summed(slice(2, 4)).astype(bf16), "gy", 1).astype(f32)
    arrived = moved(strip[:, 2:].astype(bf16), "gx", 1)
    atom_energy, forces, feature_grad = call(
        finish_kernel,
        "finish",
        [((4, 1, SLOTS), f32), ((12, 1, SLOTS), f32), ((4, SLOTS, CHAN), f32)],
        [],
        (count, pos, strip, arrived),
        8 << 10,
        10**7,
        (SMEM,),
    )
    return (
        atom_energy.reshape(species.shape),
        forces.reshape(local_pos.shape),
        feature_grad.reshape(features.shape),
    )


def solution(mesh):
    placed = (
        P("gx", "gy", "gz", None, None),
        P("gx", "gy", "gz"),
        P("gx", "gy", "gz", None),
        P("gx", "gy", "gz", None, None),
        P(),
        P(),
        P(),
        P(),
        P(),
    )
    return jax.shard_map(
        body,
        mesh=mesh,
        in_specs=placed,
        out_specs=(
            P("gx", "gy", "gz", None),
            P("gx", "gy", "gz", None, None),
            P("gx", "gy", "gz", None, None),
        ),
        check_vma=False,
    )
```
